32 devices in a mesh: section: 2 (over core), dp: 4 (over z), shard: 4 (over y, x).
Axes of the slice: x: 2, y: 2, z: 4, core: 2. Of those that a mesh axis runs over, the one named last changes fastest.
Arguments:
- tokens_in: bfloat16 [2, 2048, 768], P(None, ('dp', 'shard')), may hold values from -6 to 6
- seq_lengths: int32 [2, 16, 3], P(None, ('dp', 'shard')), may hold values from 1 to 64, 128 in all within a row
- out_grad: bfloat16 [2, 2048, 768], P(None, ('dp', 'shard')), may hold values from -6 to 6
- norm_gain: bfloat16 [2, 768], P('section', 'shard'), may hold values from 0.5 to 1.5
- w_in: bfloat16 [2, 768, 3328], P('section', 'shard'), may hold values from -0.21875 to 0.21875
- w_dt: bfloat16 [2, 768, 24], P('section', 'shard'), may hold values from -0.21875 to 0.21875
- conv_w: bfloat16 [2, 4, 1792], P('section', None, 'shard'), may hold values from -3 to 3
- conv_b: bfloat16 [2, 1792], P('section', 'shard'), may hold values from -3 to 3
- dt_bias: bfloat16 [2, 24], P('section', 'shard'), may hold values from -3 to 0
- a_log: bfloat16 [2, 24], P('section', 'shard'), may hold values from -3 to 0.5
- d_skip: bfloat16 [2, 24], P('section', 'shard'), may hold values from 0.5 to 1.5
- inner_gain: bfloat16 [2, 1536], P('section', 'shard'), may hold values from 0.5 to 1.5
- w_out: bfloat16 [2, 1536, 768], P('section', 'shard'), may hold values from -0.15625 to 0.15625
Outputs:
- section_out: bfloat16 [2, 2, 2048, 768], P('section', None, ('dp', 'shard'))
- section_in_grad: float32 [2, 2, 2048, 768], P('section', None, ('dp', 'shard'))
- g_norm_gain: float32 [2, 768], P('section', 'shard')
- g_w_in: float32 [2, 768, 3328], P('section', 'shard')
- g_w_dt: float32 [2, 768, 24], P('section', 'shard')
- g_conv_w: float32 [2, 4, 1792], P('section', None, 'shard')
- g_conv_b: float32 [2, 1792], P('section', 'shard')
- g_dt_bias: float32 [2, 24], P('section', 'shard')
- g_a_log: float32 [2, 24], P('section', 'shard')
- g_d_skip: float32 [2, 24], P('section', 'shard')
- g_inner_gain: float32 [2, 1536], P('section', 'shard')
- g_w_out: float32 [2, 1536, 768], P('section', 'shard')
The draws below stay inside these ranges and needn't reach their ends.
Inputs may be any that keep to these rules, and one draw needn't show every extreme that they name: `seq_lengths`: each row holds the lengths of the 3 sequences packed, in order, in one device's 128 tokens of a micro-batch; they sum to 128 and the longest is exactly 64.
All inputs are finite; a program needn't handle non-finite values.
Results may differ from the reference program's by a relative error of at most 0.018.
Values may be sent and summed in bfloat16 or wider, within the bound.
No kernel may reach another device: no remote copies, remote signals or barrier semaphores. Data moves between devices by JAX's collectives and lax.ppermute only.
A program may use at most 192 MiB of HBM per device.

```python
import math
import jax
import jax.numpy as jnp
import numpy as np
from jax import lax

D = 768
DI = 1536
NH = 24
CONV = 4
SPAN = 256
MICRO = 2
TOK = 128
SEQS = 3
XBC = 1792
PROJ = 3328
BLOCKS = 16
ROWS = 2048
N_SECTION = 2
N_DP = 4
N_SHARD = 4


def level_of(key, extent, cuts, least, high):
    loudness, own = 1.0, jax.random.fold_in(key, 6)
    for dim, parts in cuts:
        steps = jnp.exp(jax.random.uniform(jax.random.fold_in(own, dim), (parts,), jnp.float32, least / len(cuts), high / len(cuts)))
        loudness = loudness * jnp.repeat(steps, extent[dim] // parts).reshape([-1 if axis == dim else 1 for axis in range(len(extent))])
    return loudness


def split_up(amount, total, bound, slope):
    weights = [(1 << 20) // math.isqrt(standing ** slope) + 1 for standing in range(2, amount + 1)]
    surplus, given = total - bound - (amount - 1), [1] * (amount - 1)
    while surplus > 0:
        free = [i for i in range(amount - 1) if given[i] < bound]
        mass, budget = sum([weights[i] for i in free]), surplus
        for i in free:
            extra = min(bound - given[i], max(1, budget * weights[i] // mass), surplus)
            given[i] = given[i] + extra
            surplus = surplus - extra
    return np.array([bound] + given)


def ragged(own_key, number_of, total, most, lean):
    if number_of == 2:
        one = jax.random.randint(own_key, (), max(1, total - most), min(most, total - 1) + 1)
        return jnp.stack([one, total - one])
    lengths = jnp.asarray(split_up(number_of, total, most, lean), jnp.int32)
    twos = (number_of - 1) // 2
    source_of, receiver = lengths[1:1 + 2 * twos:2], lengths[2:2 + 2 * twos:2]
    room = jnp.minimum(source_of - 1, most - receiver)
    moved = jax.random.randint(jax.random.fold_in(own_key, 1), (twos,), 0, 1 << 20) % (room + 1)
    lengths = lengths.at[1:1 + 2 * twos:2].set(source_of - moved).at[2:2 + 2 * twos:2].set(receiver + moved)
    return lengths[jax.random.permutation(jax.random.fold_in(own_key, 2), number_of)]


def gaussian(rng, dims, spread, reach, shards=(), held_as=jnp.bfloat16):
    drawn = spread * jax.random.normal(rng, dims, jnp.float32)
    if shards:
        drawn = drawn * level_of(rng, dims, shards, -0.22, 0.18)
    return jnp.clip(drawn, -reach, reach).astype(held_as)


def setup_inputs(seed: int = 0) -> dict:
    keys = jax.random.split(jax.random.key(seed), 14)
    return {
        "tokens_in": gaussian(keys[0], (MICRO, ROWS, D), 1.0, 6.0, ((1, 16),)),
        "seq_lengths": jax.vmap(lambda own: ragged(own, SEQS, TOK, TOK // 2, 2))(jax.random.split(keys[1], MICRO * BLOCKS)).reshape((MICRO, BLOCKS, SEQS)).astype(jnp.int32),
        "out_grad": gaussian(keys[2], (MICRO, ROWS, D), 1.0, 6.0, ((1, 16),)),
        "norm_gain": jnp.clip(1.0 + 0.1 * jax.random.normal(keys[3], (N_SECTION, D), jnp.float32), 0.5, 1.5).astype(jnp.bfloat16),
        "w_in": gaussian(keys[4], (N_SECTION, D, PROJ), D ** -0.5, 0.21875, ((0, 2), (1, 4))),
        "w_dt": gaussian(keys[5], (N_SECTION, D, NH), D ** -0.5, 0.21875, ((0, 2), (1, 4))),
        "conv_w": gaussian(keys[6], (N_SECTION, CONV, XBC), 0.5, 3.0, ((0, 2), (2, 4))),
        "conv_b": gaussian(keys[7], (N_SECTION, XBC), 0.5, 3.0, ((0, 2), (1, 4))),
        "dt_bias": jnp.clip(-3.0 + 3.0 * jax.random.uniform(keys[8], (N_SECTION, NH), jnp.float32) ** level_of(keys[8], (N_SECTION, NH), ((0, 2), (1, 4)), -0.2, 0.2), -3.0, 0.0).astype(jnp.bfloat16),
        "a_log": jnp.clip(-3.0 + 3.5 * jax.random.uniform(keys[9], (N_SECTION, NH), jnp.float32) ** level_of(keys[9], (N_SECTION, NH), ((0, 2), (1, 4)), -0.2, 0.2), -3.0, 0.5).astype(jnp.bfloat16),
        "d_skip": jnp.clip(0.5 + 1.0 * jax.random.uniform(keys[10], (N_SECTION, NH), jnp.float32) ** level_of(keys[10], (N_SECTION, NH), ((0, 2), (1, 4)), -0.2, 0.2), 0.5, 1.5).astype(jnp.bfloat16),
        "inner_gain": jnp.clip(1.0 + 0.1 * jax.random.normal(keys[11], (N_SECTION, DI), jnp.float32), 0.5, 1.5).astype(jnp.bfloat16),
        "w_out": gaussian(keys[12], (N_SECTION, DI, D), DI ** -0.5, 0.15625, ((0, 2), (1, 4))),
    }


NORM_EPSILON = 1e-05

@jax.custom_vjp
def low(v):
    return lax.optimization_barrier(v.astype(jnp.bfloat16)).astype(jnp.float32)

@jax.custom_vjp
def low_back(v):
    return v

def low_keep(v):
    return (low(v), None)

def low_pass(kept, grad):
    return (grad,)

def back_keep(v):
    return (v, None)

def back_low(kept, grad):
    return (low(grad),)
low.defvjp(low_keep, low_pass)
low_back.defvjp(back_keep, back_low)

def rms_scale(values, gain_vector):
    return values * lax.rsqrt(lax.optimization_barrier(jnp.mean(values * values, axis=-1, keepdims=True)) + NORM_EPSILON) * gain_vector

def segment_ids(lengths_row, row_count):
    seq_ends = jnp.cumsum(lengths_row).astype(jnp.int32)
    positions = jnp.arange(row_count, dtype=jnp.int32)
    return lax.optimization_barrier(jnp.sum((positions[:, None] >= seq_ends[None, :]).astype(jnp.int32), axis=1)).astype(jnp.int32)

def conv_silu(conv_in, conv_taps, conv_bias, segment):
    taps = conv_taps.shape[0]
    width = conv_in.shape[1]
    conv_total = conv_bias[None, :] + conv_taps[taps - 1][None, :] * conv_in
    for offset in range(1, taps):
        shifted = jnp.concatenate([jnp.zeros((offset, width), jnp.float32), conv_in[:-offset]], axis=0)
        earlier = jnp.concatenate([jnp.full((offset,), -1, jnp.int32), segment[:-offset].astype(jnp.int32)])
        same_seg = (earlier == segment).astype(jnp.float32)[:, None]
        conv_total = conv_total + conv_taps[taps - 1 - offset][None, :] * shifted * same_seg
    return jax.nn.silu(conv_total)

def scan_heads(head_in, in_state, out_state, step_size, decay_log, segment, span_len):
    length, heads, head_width = head_in.shape
    state_width = in_state.shape[1]
    block_len = min(length, span_len)
    count = length // block_len
    span_data = (head_in.reshape(count, block_len, heads, head_width), in_state.reshape(count, block_len, state_width), out_state.reshape(count, block_len, state_width), step_size.reshape(count, block_len, heads), decay_log.reshape(count, block_len, heads), segment.astype(jnp.int32).reshape(count, block_len))
    highest = lax.Precision.HIGHEST

    def span_step(carry, pieces):
        carried, prev_seg = carry
        part_x, part_b, part_c, part_step, part_log, part_seg = pieces
        cumulative = jnp.cumsum(part_log, axis=0)
        positions = jnp.arange(block_len, dtype=jnp.int32)
        causal_mask = ((part_seg[:, None] == part_seg[None, :]) & (positions[:, None] >= positions[None, :])).astype(jnp.float32)[:, :, None]
        decay = jnp.exp((cumulative[:, None, :] - cumulative[None, :, :]) * causal_mask) * causal_mask
        scores = jnp.dot(part_c, part_b.T, precision=highest)
        weights = decay * (scores[:, :, None] * part_step[None, :, :])
        result = jnp.einsum('ijh,jhp->ihp', weights, part_x, precision=highest)
        entering = (part_seg == prev_seg).astype(jnp.float32)[:, None] * jnp.exp(cumulative)
        result = result + entering[:, :, None] * jnp.einsum('in,hpn->ihp', part_c, carried, precision=highest)
        last_seg = part_seg[-1].astype(jnp.int32)
        tail_weight = jnp.exp(cumulative[-1][None, :] - cumulative) * (part_seg == last_seg).astype(jnp.float32)[:, None] * part_step
        passing = (last_seg == prev_seg).astype(jnp.float32) * jnp.exp(cumulative[-1])
        new_state = jnp.einsum('jh,jn,jhp->hpn', tail_weight, part_b, part_x, precision=highest) + passing[:, None, None] * carried
        return ((new_state, last_seg), result)
    start = (jnp.zeros((heads, head_width, state_width), jnp.float32), jnp.full((), -1, jnp.int32))
    unused, results = lax.scan(jax.checkpoint(span_step), start, span_data)
    return results.reshape(length, heads, head_width)

def mix(projected, dt_raw, small_params, segment, span_len):
    conv_taps, conv_bias, step_bias, rate_log, skip_coef, gate_gain = small_params
    inner = gate_gain.shape[0]
    heads = step_bias.shape[0]
    state_width = (projected.shape[1] - 2 * inner) // 2
    gate_part = projected[:, :inner]
    conv_out = conv_silu(projected[:, inner:], conv_taps, conv_bias, segment)
    head_in = conv_out[:, :inner].reshape(-1, heads, inner // heads)
    in_state = conv_out[:, inner:inner + state_width]
    out_state = conv_out[:, inner + state_width:]
    step_size = jax.nn.softplus(dt_raw + step_bias[None, :])
    decay_log = -step_size * jnp.exp(rate_log)[None, :]
    scanned = scan_heads(head_in, in_state, out_state, step_size, decay_log, segment, span_len)
    scanned = scanned + skip_coef[None, :, None] * head_in
    gated = scanned.reshape(-1, inner) * jax.nn.silu(gate_part)
    return rms_scale(gated, gate_gain)

def layer(values, params, segment):
    highest = lax.Precision.HIGHEST
    normed = low(rms_scale(values, params[0]))
    projected = low_back(jnp.dot(normed, params[1], precision=highest))
    dt_raw = low_back(jnp.dot(normed, params[2], precision=highest))
    mixed = low(mix(projected, dt_raw, params[3:9], segment, SPAN))
    return values + low_back(jnp.dot(mixed, params[9], precision=highest))

def forward(group_in, probe, params_all, segments):
    first_params = tuple((piece[0] for piece in params_all))
    second_params = tuple((piece[1] for piece in params_all))
    hidden = low(jax.vmap(layer, in_axes=(0, None, 0))(group_in, first_params, segments))
    second_in = low_back(hidden) + probe
    final = jax.vmap(layer, in_axes=(0, None, 0))(second_in, second_params, segments)
    return (hidden, final)

def reference(tokens_in, seq_lengths, out_grad, norm_gain, w_in, w_dt, conv_w, conv_b, dt_bias, a_log, d_skip, inner_gain, w_out):
    params_all = tuple((piece.astype(jnp.float32) for piece in (norm_gain, w_in, w_dt, conv_w, conv_b, dt_bias, a_log, d_skip, inner_gain, w_out)))
    groups = MICRO * N_DP
    group_x = tokens_in.astype(jnp.float32).reshape(groups, N_SHARD, TOK, D)
    group_cot = out_grad.astype(jnp.float32).reshape(groups, N_SHARD, TOK, D)
    group_len = seq_lengths.astype(jnp.int32).reshape(groups, N_SHARD, SEQS)

    def one_group(accum, data):
        group_in, group_back, group_lengths = data
        segments = jax.vmap(lambda row_lengths: segment_ids(row_lengths, TOK))(group_lengths)
        probe = jnp.zeros_like(group_in)
        outputs, pullback = jax.vjp(lambda first_in, probe_in, weights: forward(first_in, probe_in, weights, segments), group_in, probe, params_all)
        grad_in, grad_mid, grad_params = pullback((jnp.zeros_like(outputs[0]), group_back))
        accum = tuple((total + piece for total, piece in zip(accum, grad_params)))
        return (accum, (outputs[0].astype(jnp.bfloat16), outputs[1].astype(jnp.bfloat16), grad_in, grad_mid))
    start = tuple((jnp.zeros_like(piece) for piece in params_all))
    grads, (hidden_all, final_all, grad_first, grad_second) = lax.scan(one_group, start, (group_x, group_cot, group_len))
    full_shape = (MICRO, N_DP * N_SHARD * TOK, D)
    section_out = jnp.stack([hidden_all.reshape(full_shape), final_all.reshape(full_shape)])
    section_in_grad = jnp.stack([grad_first.reshape(full_shape), grad_second.reshape(full_shape)])
    return (section_out, section_in_grad, grads[0], grads[1], grads[2], grads[3], grads[4], grads[5], grads[6], grads[7], grads[8], grads[9])
```

```python
import functools

import jax
import jax.numpy as jnp
from jax import lax
from jax.experimental import pallas as pl
from jax.experimental.pallas import tpu as pltpu
from jax.sharding import PartitionSpec as P

EPS = 1e-05
F32 = jnp.float32
BF16 = jnp.bfloat16
LANES = 128
CHUNK = 256
VMEM_LIMIT = 56 * 2**20


def nn(a, b):
    return jnp.dot(a, b, preferred_element_type=F32)


def nt(a, b):
    return lax.dot_general(a, b, (((1,), (1,)), ((), ())), preferred_element_type=F32)


def tn(a, b):
    return lax.dot_general(a, b, (((0,), (0,)), ((), ())), preferred_element_type=F32)


def split2(v):
    hi = v.astype(BF16)
    return hi, (v - hi.astype(F32)).astype(BF16)


def split3(v):
    hi, rest = v.astype(BF16), None
    rest = v - hi.astype(F32)
    mid = rest.astype(BF16)
    return hi, mid, (rest - mid.astype(F32)).astype(BF16)


def softplus(v):
    return jnp.maximum(v, 0.0) + jnp.log1p(jnp.exp(-jnp.abs(v)))


def sigmoid(v):
    return 1.0 / (1.0 + jnp.exp(-v))


class Layer:
    def __init__(self, tok, width, inner, convolved, heads, taps):
        self.tok, self.width, self.inner, self.convolved = tok, width, inner, convolved
        self.heads, self.taps = heads, taps
        self.head_width = inner // heads
        self.state = (convolved - inner) // 2
        self.proj = inner + convolved

    def scratch(self, backward, micro):
        t, d, i, c = self.tok, self.width, self.inner, self.convolved
        shapes = [
            pltpu.VMEM((d, self.proj), BF16),
            pltpu.VMEM((i, d), BF16),
            pltpu.VMEM((LANES, i), BF16),
            pltpu.VMEM((t, self.proj), F32),
            pltpu.VMEM((t, c), F32),
            pltpu.VMEM((t, i), BF16),
            pltpu.VMEM((t, i), F32),
            pltpu.VMEM((t, i), F32),
            pltpu.VMEM((t, i), BF16),
        ]
        if backward:
            shapes += [
                pltpu.VMEM((t, c), F32),
                pltpu.VMEM((self.heads, t, t), F32),
                pltpu.VMEM((t, i), F32),
                pltpu.VMEM((t, i), F32),
                pltpu.VMEM((t, c), F32),
                pltpu.VMEM((t, i), F32),
                pltpu.VMEM((t, i), F32),
                pltpu.VMEM((d, micro * t), BF16),
                pltpu.VMEM((i, micro * t), BF16),
                pltpu.VMEM((micro * t, self.proj), BF16),
                pltpu.VMEM((micro * t, LANES), BF16),
            ]
        return shapes

    def masks(self, lens_ref, m):
        t = self.tok
        row = lax.broadcasted_iota(jnp.int32, (t, t), 0)
        col = lax.broadcasted_iota(jnp.int32, (t, t), 1)
        token = lax.broadcasted_iota(jnp.int32, (t, 1), 0)
        seg_row = jnp.zeros((t, t), jnp.int32)
        seg_col = jnp.zeros((t, t), jnp.int32)
        segs = [jnp.zeros((t, 1), jnp.int32) for _ in range(self.taps)]
        end = jnp.int32(0)
        for s in range(lens_ref.shape[1]):
            end = end + lens_ref[m, s]
            seg_row = seg_row + jnp.where(row >= end, 1, 0)
            seg_col = seg_col + jnp.where(col >= end, 1, 0)
            segs = [v + jnp.where(token - k >= end, 1, 0) for k, v in enumerate(segs)]
        causal = (row >= col) & (seg_row == seg_col)
        tri = jnp.where(row >= col, 1.0, 0.0).astype(BF16)
        keep = [
            jnp.where((token >= k) & (segs[k] == segs[0]), 1.0, 0.0) for k in range(self.taps)
        ]
        return causal, tri, keep

    def forward(self, u, w, prm, s, masks):
        chan, heads_prm, w_dt = prm
        causal, tri, keep = masks
        t, inner, taps = self.tok, self.inner, self.taps
        rs = lax.rsqrt(jnp.mean(u * u, axis=-1, keepdims=True) + EPS)
        q = u * rs
        normed = (q * chan[6:7, : self.width]).astype(BF16)
        for c in range(0, self.proj, CHUNK):
            s["proj"][:, c : c + CHUNK] = nn(normed, w["in"][:, c : c + CHUNK])
        dtv = nn(normed, w_dt[...]) + heads_prm[0:1, :]
        step = softplus(dtv)
        rate = jnp.exp(heads_prm[1:2, :])
        la = -step * rate
        cum = sum(nn(tri, part) for part in split3(la))
        cum_t = cum.T
        for c in range(0, self.convolved, CHUNK):
            cols = slice(c, c + CHUNK)
            ci = s["proj"][:, inner + c : inner + c + CHUNK]
            pre = chan[taps : taps + 1, cols] + chan[taps - 1 : taps, cols] * ci
            for k in range(1, taps):
                pre = pre + chan[taps - 1 - k : taps - k, cols] * (
                    pltpu.roll(ci, k, 0) * keep[k]
                )
            if "pre" in s:
                s["pre"][:, cols] = pre
            s["co"][:, cols] = pre * sigmoid(pre)
        bm = s["co"][:, inner : inner + self.state].astype(BF16)
        cm = s["co"][:, inner + self.state : inner + 2 * self.state].astype(BF16)
        scores = nt(cm, bm)
        step_hi, step_lo = split2(step)
        for c in range(0, inner, CHUNK):
            cols = slice(c, c + CHUNK)
            spread = nn(step_hi, s["e"][:, cols]) + nn(step_lo, s["e"][:, cols])
            if "stepx" in s:
                s["stepx"][:, cols] = spread
            s["xs"][:, cols] = (s["co"][:, cols] * spread).astype(BF16)
        low_half = lax.broadcasted_iota(jnp.int32, (t, LANES), 1) < self.head_width
        for pair in range(inner // LANES):
            cols = slice(pair * LANES, (pair + 1) * LANES)
            parts = []
            for h in (2 * pair, 2 * pair + 1):
                gap = jnp.where(causal, cum[:, h : h + 1] - cum_t[h : h + 1, :], -1e30)
                decay = jnp.exp(gap)
                if "decay" in s:
                    s["decay"][h] = decay
                parts.append((decay * scores).astype(BF16))
            xs = s["xs"][:, cols].astype(F32)
            blocks = jnp.concatenate(
                [jnp.where(low_half, xs, 0.0).astype(BF16), jnp.where(low_half, 0.0, xs).astype(BF16)],
                axis=0,
            )
            s["ys"][:, cols] = nn(jnp.concatenate(parts, axis=1), blocks)
        total = jnp.zeros((t, 1), F32)
        for c in range(0, inner, CHUNK):
            cols = slice(c, c + CHUNK)
            z = s["proj"][:, cols]
            y = s["ys"][:, cols] + chan[7:8, cols] * s["co"][:, cols]
            gated = y * (z * sigmoid(z))
            s["gated"][:, cols] = gated
            total = total + jnp.sum(gated * gated, axis=-1, keepdims=True)
        r = lax.rsqrt(total * (1.0 / inner) + EPS)
        for c in range(0, inner, CHUNK):
            cols = slice(c, c + CHUNK)
            s["mixed"][:, cols] = (s["gated"][:, cols] * r * chan[5:6, cols]).astype(BF16)
        out = u + nn(s["mixed"][...], w["out"][...])
        return out, dict(
            rs=rs, q=q, normed=normed, dtv=dtv, step=step, rate=rate, la=la,
            bm=bm, cm=cm, scores=scores, r=r, low_half=low_half,
        )

    def backward(self, dres, kept, w, prm, s, masks, small, rows, lanes):
        chan, heads_prm, w_dt = prm
        causal, tri, keep = masks
        t, inner, taps = self.tok, self.inner, self.taps
        dout = dres
        r, low_half = kept["r"], kept["low_half"]
        s["normed_t"][:, lanes] = kept["normed"].astype(F32).T.astype(BF16)
        dot_total = jnp.zeros((t, 1), F32)
        for c in range(0, inner, CHUNK):
            cols = slice(c, c + CHUNK)
            s["mixed_t"][cols, lanes] = s["mixed"][:, cols].astype(F32).T.astype(BF16)
            dm = nt(dout, w["out"][cols, :])
            ghat = s["gated"][:, cols] * r
            prod = dm * ghat
            small[5:6, cols] += jnp.sum(prod, axis=0, keepdims=True)
            dgh = dm * chan[5:6, cols]
            dot_total = dot_total + jnp.sum(dgh * ghat, axis=-1, keepdims=True)
            s["dy"][:, cols] = dgh
        mean_dot = dot_total * (1.0 / inner)
        for c in range(0, inner, CHUNK):
            cols = slice(c, c + CHUNK)
            x = s["co"][:, cols]
            dgated = r * (s["dy"][:, cols] - s["gated"][:, cols] * (r * mean_dot))
            z = s["proj"][:, cols]
            sg = sigmoid(z)
            y = s["ys"][:, cols] + chan[7:8, cols] * x
            dy = dgated * (z * sg)
            s["dproj"][rows, cols] = (dgated * y * (sg * (1.0 + z * (1.0 - sg)))).astype(BF16)
            s["dy"][:, cols] = dy
            small[7:8, cols] += jnp.sum(dy * x, axis=0, keepdims=True)
        ds = jnp.zeros((t, t), F32)
        scores = kept["scores"]
        for pair in range(inner // LANES):
            cols = slice(pair * LANES, (pair + 1) * LANES)
            h = 2 * pair
            dy = s["dy"][:, cols]
            dyb = dy.astype(BF16)
            dyr = dyb.astype(F32)
            xsb = s["xs"][:, cols]
            stacked = jnp.concatenate(
                [jnp.where(low_half, dyr, 0.0).astype(BF16), jnp.where(low_half, 0.0, dyr).astype(BF16)],
                axis=0,
            )
            dw = nt(stacked, xsb)
            decay0, decay1 = s["decay"][h], s["decay"][h + 1]
            ds = ds + dw[:t] * decay0 + dw[t:] * decay1
            weights = jnp.concatenate(
                [(decay0 * scores).astype(BF16), (decay1 * scores).astype(BF16)], axis=0
            )
            dxs = tn(weights, stacked)
            x = s["co"][:, cols]
            s["dco"][:, cols] = dxs * s["stepx"][:, cols] + chan[7:8, cols] * dy
            s["t1"][:, cols] = dyr * s["ys"][:, cols] - dxs * xsb.astype(F32)
            s["t2"][:, cols] = dxs * x
        dcum = sum(nt(part, s["e"][...]) for part in split2(s["t1"][...]))
        dstep = sum(nt(part, s["e"][...]) for part in split2(s["t2"][...]))
        dla = sum(tn(tri, part) for part in split3(dcum))
        dstep = dstep - kept["rate"] * dla
        ddt = dstep * sigmoid(kept["dtv"])
        small[8:9, 0:LANES] += jnp.sum(ddt, axis=0, keepdims=True)
        small[9:10, 0:LANES] += jnp.sum(dla * kept["la"], axis=0, keepdims=True)
        ddtb = ddt.astype(BF16)
        s["ddt"][rows, :] = ddtb
        dsb = ds.astype(BF16)
        s["dco"][:, inner : inner + self.state] = tn(dsb, kept["cm"])
        s["dco"][:, inner + self.state : inner + 2 * self.state] = nn(dsb, kept["bm"])
        for c in range(0, self.convolved, CHUNK):
            cols = slice(c, c + CHUNK)
            ci = s["proj"][:, inner + c : inner + c + CHUNK]
            pre = s["pre"][:, cols]
            sg = sigmoid(pre)
            dpre = s["dco"][:, cols] * (sg * (1.0 + pre * (1.0 - sg)))
            small[taps : taps + 1, cols] += jnp.sum(dpre, axis=0, keepdims=True)
            small[taps - 1 : taps, cols] += jnp.sum(dpre * ci, axis=0, keepdims=True)
            dci = chan[taps - 1 : taps, cols] * dpre
            for k in range(1, taps):
                back = dpre * keep[k]
                small[taps - 1 - k : taps - k, cols] += jnp.sum(
                    back * pltpu.roll(ci, k, 0), axis=0, keepdims=True
                )
                dci = dci + chan[taps - 1 - k : taps - k, cols] * pltpu.roll(back, t - k, 0)
            s["dproj"][rows, inner + c : inner + c + CHUNK] = dci.astype(BF16)
        dnormed = nt(s["dproj"][rows, :], w["in"][...]) + nt(ddtb, w_dt[...])
        q, rs = kept["q"], kept["rs"]
        small[6:7, : self.width] += jnp.sum(dnormed * q, axis=0, keepdims=True)
        dq = dnormed * chan[6:7, : self.width]
        return dres.astype(F32) + rs * (dq - q * jnp.mean(dq * q, axis=-1, keepdims=True))


NAMES = ("e", "proj", "co", "xs", "ys", "gated", "mixed")
BACK_NAMES = ("pre", "decay", "stepx", "dy", "dco", "t1", "t2", "normed_t", "mixed_t", "dproj", "ddt")
SMALL_ROWS = 16


def load_weights(n, in_refs, out_refs, w, sems, me):
    copies = []
    for k in range(n):
        owner = lax.bitwise_xor(me, k)
        for which, (ref, dst) in enumerate(((in_refs[k], w["in"]), (out_refs[k], w["out"]))):
            size = ref.shape[0]
            start = pl.multiple_of(owner * size, size)
            copies.append(
                pltpu.make_async_copy(ref, dst.at[pl.ds(start, size), :], sems.at[which, k])
            )
    for copy in copies:
        copy.start()
    for copy in copies:
        copy.wait()


def fill_spread(layer, ref):
    head = lax.broadcasted_iota(jnp.int32, ref.shape, 0) * layer.head_width
    lane = lax.broadcasted_iota(jnp.int32, ref.shape, 1)
    ref[...] = jnp.where((lane >= head) & (lane < head + layer.head_width), 1.0, 0.0).astype(BF16)


def forward_kernel(layer, micro, n, section, *refs):
    lens, u_ref, chan, heads_prm, w_dt = refs[:5]
    in_refs, out_refs = refs[5 : 5 + n], refs[5 + n : 5 + 2 * n]
    y_ref = refs[5 + 2 * n]
    w_in, w_out, *scr = refs[6 + 2 * n : -1]
    sems = refs[-1]
    s = dict(zip(NAMES, scr))
    w = {"in": w_in, "out": w_out}

    @pl.when(lax.axis_index("section") == section)
    def _():
        load_weights(n, in_refs, out_refs, w, sems, lax.axis_index("shard"))
        fill_spread(layer, s["e"])

        @pl.loop(0, micro)
        def _(m):
            rows = pl.ds(pl.multiple_of(m * layer.tok, layer.tok), layer.tok)
            out, _ = layer.forward(
                u_ref[rows, :].astype(F32), w, (chan, heads_prm, w_dt), s, layer.masks(lens, m)
            )
            y_ref[rows, :] = out.astype(BF16)


def both_kernel(layer, micro, n, section, *refs):
    lens, u_ref, chan, heads_prm, w_dt, dres_ref = refs[:6]
    in_refs, out_refs = refs[6 : 6 + n], refs[6 + n : 6 + 2 * n]
    y_ref, din_ref, small, gdt_ref = refs[6 + 2 * n : 10 + 2 * n]
    gin_refs = refs[10 + 2 * n : 10 + 3 * n]
    gout_refs = refs[10 + 3 * n : 10 + 4 * n]
    w_in, w_out, *scr, gin_buf, gout_buf, sems, gsems = refs[10 + 4 * n :]
    s = dict(zip(NAMES + BACK_NAMES, scr))
    w = {"in": w_in, "out": w_out}

    @pl.when(lax.axis_index("section") == section)
    def _():
        me = lax.axis_index("shard")
        load_weights(n, in_refs, out_refs, w, sems, me)
        fill_spread(layer, s["e"])
        small[...] = jnp.zeros(small.shape, F32)

        @pl.loop(0, micro)
        def _(m):
            start = pl.multiple_of(m * layer.tok, layer.tok)
            rows = pl.ds(start, layer.tok)
            prm = (chan, heads_prm, w_dt)
            masks = layer.masks(lens, m)
            out, kept = layer.forward(u_ref[rows, :].astype(F32), w, prm, s, masks)
            y_ref[rows, :] = out.astype(BF16)
            din_ref[rows, :] = layer.backward(
                dres_ref[rows, :], kept, w, prm, s, masks, small, rows, rows
            )

        gdt_ref[...] = nn(s["normed_t"][...], s["ddt"][...])
        out_rows, in_rows = gout_buf.shape[1], gin_buf.shape[1]

        def send_off(which, j, buf, targets):
            for k in range(n):

                @pl.when(lax.bitwise_xor(me, k) == j)
                def _(k=k):
                    pltpu.make_async_copy(buf.at[j], targets[k], gsems.at[which, k]).start()

        for j in range(n):
            part = slice(j * out_rows, (j + 1) * out_rows)
            gout_buf[j] = nn(s["mixed_t"][part, :], dres_ref[...]).astype(BF16)
            send_off(1, j, gout_buf, gout_refs)
        for j in range(n):
            part = slice(j * in_rows, (j + 1) * in_rows)
            for c in range(0, layer.proj, CHUNK):
                gin_buf[j, :, c : c + CHUNK] = nn(
                    s["normed_t"][part, :], s["dproj"][:, c : c + CHUNK]
                ).astype(BF16)
            send_off(0, j, gin_buf, gin_refs)
        for k in range(n):
            pltpu.make_async_copy(gin_buf.at[k], gin_refs[k], gsems.at[0, k]).wait()
            pltpu.make_async_copy(gout_buf.at[k], gout_refs[k], gsems.at[1, k]).wait()


def call_layer(layer, micro, section, backward, lens, u, prm, pieces_in, pieces_out, dres=None):
    n = len(pieces_in)
    tokens = micro * layer.tok
    vmem, hbm = pl.BlockSpec(memory_space=pltpu.VMEM), pl.BlockSpec(memory_space=pl.ANY)
    smem = pl.BlockSpec(memory_space=pltpu.SMEM)
    scratch = layer.scratch(backward, micro)
    y = jax.ShapeDtypeStruct((tokens, layer.width), BF16)
    work = 2 * tokens * layer.width * (layer.proj + layer.inner)
    cost = pl.CostEstimate(
        flops=work * (4 if backward else 1),
        bytes_accessed=8_000_000 * (2 if backward else 1),
        transcendentals=tokens * layer.tok * layer.heads,
    )
    params = pltpu.CompilerParams(vmem_limit_bytes=VMEM_LIMIT)
    load_sems = pltpu.SemaphoreType.DMA((2, n))
    if not backward:
        return pl.pallas_call(
            functools.partial(forward_kernel, layer, micro, n, section),
            out_shape=y,
            in_specs=[smem] + [vmem] * 4 + [hbm] * (2 * n),
            out_specs=vmem,
            scratch_shapes=scratch + [load_sems],
            compiler_params=params,
            cost_estimate=cost,
            name="layer_forward",
        )(lens, u, *prm, *pieces_in, *pieces_out)
    piece_in, piece_out = pieces_in[0].shape, pieces_out[0].shape
    return pl.pallas_call(
        functools.partial(both_kernel, layer, micro, n, section),
        out_shape=[
            y,
            jax.ShapeDtypeStruct((tokens, layer.width), F32),
            jax.ShapeDtypeStruct((SMALL_ROWS, layer.convolved), F32),
            jax.ShapeDtypeStruct((layer.width, LANES), F32),
        ]
        + [jax.ShapeDtypeStruct(piece_in, BF16)] * n
        + [jax.ShapeDtypeStruct(piece_out, BF16)] * n,
        in_specs=[smem] + [vmem] * 5 + [hbm] * (2 * n),
        out_specs=[vmem] * 4 + [hbm] * (2 * n),
        scratch_shapes=scratch
        + [
            pltpu.VMEM((n,) + piece_in, BF16),
            pltpu.VMEM((n,) + piece_out, BF16),
            load_sems,
            pltpu.SemaphoreType.DMA((2, n)),
        ],
        compiler_params=params,
        cost_estimate=cost,
        name="layer_both",
    )(lens, u, *prm, dres, *pieces_in, *pieces_out)


def exchange(block, axis, distance, section=None):
    size = lax.axis_size(axis)
    if section is None:
        return lax.ppermute(block, axis, [(i, i ^ distance) for i in range(size)])
    base = section * size
    route = [(base + i, base + (i ^ distance)) for i in range(size)]
    return lax.ppermute(block, ("section", axis), route)


def wide_sum(*parts):
    return sum(part.astype(F32) for part in parts)


def gather_pieces(shards, section):
    n = lax.axis_size("shard")
    return tuple(
        [shard] + [exchange(shard, "shard", k, section) for k in range(1, n)] for shard in shards
    )


def sum_over_dp(block, section):
    size = lax.axis_size("dp")
    me = lax.axis_index("dp")
    steps = []
    distance = 1
    while distance < size:
        half = block.shape[0] // 2
        upper = (me & distance) != 0
        first, second = block[:half], block[half:]
        got = exchange(jnp.where(upper, first, second), "dp", distance, section)
        block = wide_sum(jnp.where(upper, second, first), got).astype(BF16)
        steps.append((distance, upper))
        distance *= 2
    for distance, upper in reversed(steps):
        got = exchange(block, "dp", distance, section)
        block = jnp.concatenate([jnp.where(upper, got, block), jnp.where(upper, block, got)], axis=0)
    return block


def sum_small(block):
    n = lax.axis_size("shard")
    total = wide_sum(block[0], *[exchange(block[k], "shard", k) for k in range(1, n)])
    distance = 1
    while distance < lax.axis_size("dp"):
        total = total + exchange(total, "dp", distance)
        distance *= 2
    return total


def reduce_layer(pieces, section):
    n = len(pieces)
    got = [exchange(pieces[k], "shard", k, section) for k in range(1, n)]
    return sum_over_dp(wide_sum(pieces[0], *got).astype(BF16), section)


def after(value, token):
    return lax.optimization_barrier((value, token))[0]


def body(
    tokens_in, seq_lengths, out_grad, norm_gain, w_in, w_dt, conv_w, conv_b,
    dt_bias, a_log, d_skip, inner_gain, w_out,
):
    is_first = lax.axis_index("section") == 0
    shard_pos = lax.axis_index("shard")
    n = lax.axis_size("shard")
    micro, tok, width = tokens_in.shape
    own_heads = dt_bias.shape[1]
    heads, taps = own_heads * n, conv_w.shape[1]
    inner, convolved = inner_gain.shape[1] * n, conv_b.shape[1] * n
    layer = Layer(tok, width, inner, convolved, heads, taps)

    own_conv, own_inner, own_width = conv_b.shape[1], inner_gain.shape[1], norm_gain.shape[1]
    flat = jnp.concatenate(
        [v.reshape(-1) for v in (conv_w, conv_b, inner_gain, norm_gain, dt_bias, a_log, d_skip, w_dt)]
    )
    packed = -(-flat.shape[0] // 2048) * 2048
    flat = jnp.pad(flat, (0, packed - flat.shape[0])).reshape(-1, LANES)
    everyone = lax.all_gather(flat, "shard").reshape(n, packed)

    at = [0]

    def take(count):
        at[0] += count
        return everyone[:, at[0] - count : at[0]]

    conv_w_all = take(taps * own_conv).reshape(n, taps, own_conv).transpose(1, 0, 2).reshape(taps, convolved)
    conv_b_all = take(own_conv).reshape(1, convolved)
    inner_all = take(own_inner).reshape(1, inner)
    norm_all = take(own_width).reshape(1, width)
    dt_bias_all = take(own_heads).reshape(1, heads)
    a_log_all = take(own_heads).reshape(1, heads)
    d_skip_all = take(own_heads).reshape(1, heads)
    w_dt_all = jnp.pad(take(own_width * heads).reshape(width, heads), ((0, 0), (0, LANES - heads)))

    def padded(row):
        return jnp.pad(row, ((0, 0), (0, convolved - row.shape[1])))

    skip_all = jnp.repeat(d_skip_all, inner // heads, axis=1)
    chan = jnp.concatenate(
        [conv_w_all, conv_b_all, padded(inner_all), padded(norm_all), padded(skip_all)], axis=0
    ).astype(F32)
    heads_prm = jnp.pad(
        jnp.concatenate([dt_bias_all, a_log_all], axis=0), ((0, 6), (0, LANES - heads))
    ).astype(F32)
    prm = (chan, heads_prm, w_dt_all)

    shards = (w_in[0], w_out[0])
    first_w = gather_pieces(shards, 0)
    token = sum(
        piece[-1:, -LANES:].astype(F32) for group in first_w for piece in group[1:]
    ).astype(BF16)
    token = lax.ppermute(token, "section", [(0, 1)])
    second_w = gather_pieces(after(shards, token), 1)

    lens = seq_lengths[:, 0, :]
    tokens = tokens_in.reshape(micro * tok, width)
    cotangent = out_grad.reshape(micro * tok, width)
    hidden = call_layer(layer, micro, 0, False, lens, tokens, prm, *first_w)
    arrived = lax.ppermute(hidden, "section", [(0, 1)])
    final, second_in_grad, second_small, second_dt, *second_g = call_layer(
        layer, micro, 1, True, lens, arrived, prm, *second_w, dres=cotangent
    )
    back = lax.ppermute(second_in_grad.astype(BF16), "section", [(1, 0)])
    _, first_in_grad, first_small, first_dt, *first_g = call_layer(
        layer, micro, 0, True, lens, tokens, prm, *first_w, dres=back
    )
    second_done = [reduce_layer(second_g[n:], 1), reduce_layer(second_g[:n], 1)]
    first_done = [reduce_layer(first_g[n:], 0), reduce_layer(first_g[:n], 0)]
    g_w_out, g_w_in = [
        jnp.where(is_first, a, b).astype(F32)[None] for a, b in zip(first_done, second_done)
    ]

    small = jnp.where(is_first, first_small, second_small)
    small_dt = jnp.where(is_first, first_dt, second_dt)
    skip = small[7, :inner].reshape(heads, -1).sum(axis=1)
    rows = (
        small[:taps].reshape(taps, n, own_conv).transpose(1, 0, 2).reshape(n, -1),
        small[taps].reshape(n, own_conv),
        small[5, :inner].reshape(n, own_inner),
        small[6, :width].reshape(n, own_width),
        small[8, :heads].reshape(n, own_heads),
        small[9, :heads].reshape(n, own_heads),
        skip.reshape(n, own_heads),
        small_dt[:, :heads].reshape(n, -1),
    )
    by_shard = jnp.concatenate(rows, axis=1)
    by_shard = jnp.pad(by_shard, ((0, 0), (0, packed - by_shard.shape[1]))).reshape(n, -1, LANES)
    by_distance = jnp.stack(
        [lax.dynamic_index_in_dim(by_shard, shard_pos ^ k, 0, keepdims=False) for k in range(n)]
    )
    done = sum_small(by_distance).reshape(packed)
    at[0] = 0

    def cut(*shape):
        count = 1
        for extent in shape:
            count *= extent
        at[0] += count
        return done[at[0] - count : at[0]].reshape(shape)

    g_conv_w, g_conv_b = cut(1, taps, own_conv), cut(1, own_conv)
    g_inner, g_norm = cut(1, own_inner), cut(1, own_width)
    g_dt_bias, g_a_log, g_d_skip = cut(1, own_heads), cut(1, own_heads), cut(1, own_heads)
    g_w_dt = cut(1, own_width, heads)

    shape = (1, micro, tok, width)
    section_out = jnp.where(is_first, hidden, final).reshape(shape)
    section_in_grad = jnp.where(is_first, first_in_grad, second_in_grad).reshape(shape)
    return (
        section_out, section_in_grad, g_norm, g_w_in, g_w_dt, g_conv_w, g_conv_b,
        g_dt_bias, g_a_log, g_d_skip, g_inner, g_w_out,
    )


def solution(mesh):
    spread = P(None, ("dp", "shard"), None)
    flat, tall, conv = P("section", "shard"), P("section", "shard", None), P("section", None, "shard")
    outer = P("section", None, ("dp", "shard"), None)
    return jax.shard_map(
        body,
        mesh=mesh,
        in_specs=(spread, spread, spread, flat, tall, tall, conv, flat, flat, flat, flat, flat, tall),
        out_specs=(outer, outer, flat, tall, tall, conv, flat, flat, flat, flat, flat, tall),
        check_vma=False,
    )
```

```python
import functools
from typing import NamedTuple

import jax
import jax.numpy as jnp
from jax import lax
from jax.experimental import pallas as pl
from jax.experimental.pallas import tpu as pltpu
from jax.sharding import PartitionSpec as P

EPS = 1e-05
F32 = jnp.float32
BF16 = jnp.bfloat16
LANES = 128
CHUNK = 256
VMEM_LIMIT = 56 * 2**20


def nn(a, b):
    return jnp.dot(a, b, preferred_element_type=F32)


def nt(a, b):
    return lax.dot_general(a, b, (((1,), (1,)), ((), ())), preferred_element_type=F32)


def tn(a, b):
    return lax.dot_general(a, b, (((0,), (0,)), ((), ())), preferred_element_type=F32)


def split2(v):
    hi = v.astype(BF16)
    return hi, (v - hi.astype(F32)).astype(BF16)


def split3(v):
    hi, rest = v.astype(BF16), None
    rest = v - hi.astype(F32)
    mid = rest.astype(BF16)
    return hi, mid, (rest - mid.astype(F32)).astype(BF16)


def softplus(v):
    return jnp.maximum(v, 0.0) + jnp.log1p(jnp.exp(-jnp.abs(v)))


def sigmoid(v):
    return 1.0 / (1.0 + jnp.exp(-v))


class Layer:
    def __init__(self, tok, width, inner, convolved, heads, taps):
        self.tok, self.width, self.inner, self.convolved = tok, width, inner, convolved
        self.heads, self.taps = heads, taps
        self.head_width = inner // heads
        self.state = (convolved - inner) // 2
        self.proj = inner + convolved

    def scratch(self, backward, micro):
        t, d, i, c = self.tok, self.width, self.inner, self.convolved
        shapes = [
            pltpu.VMEM((d, self.proj), BF16),
            pltpu.VMEM((i, d), BF16),
            pltpu.VMEM((LANES, i), BF16),
            pltpu.VMEM((t, self.proj), F32),
            pltpu.VMEM((t, c), F32),
            pltpu.VMEM((t, i), BF16),
            pltpu.VMEM((t, i), F32),
            pltpu.VMEM((t, i), F32),
            pltpu.VMEM((t, i), BF16),
        ]
        if backward:
            shapes += [
                pltpu.VMEM((t, c), F32),
                pltpu.VMEM((self.heads, t, t), F32),
                pltpu.VMEM((t, i), F32),
                pltpu.VMEM((t, i), F32),
                pltpu.VMEM((t, c), F32),
                pltpu.VMEM((t, i), F32),
                pltpu.VMEM((t, i), F32),
                pltpu.VMEM((d, micro * t), BF16),
                pltpu.VMEM((i, micro * t), BF16),
                pltpu.VMEM((micro * t, self.proj), BF16),
                pltpu.VMEM((micro * t, LANES), BF16),
            ]
        return shapes

    def blocks(self, n):
        matrices = (self.width // n * self.proj + self.inner // n * self.width) // (self.width // n * CHUNK)
        return -(-(matrices + 1) // (2 * CHUNKS)) * 2 * CHUNKS

    def masks(self, lens_ref, m):
        t = self.tok
        row = lax.broadcasted_iota(jnp.int32, (t, t), 0)
        col = lax.broadcasted_iota(jnp.int32, (t, t), 1)
        token = lax.broadcasted_iota(jnp.int32, (t, 1), 0)
        seg_row = jnp.zeros((t, t), jnp.int32)
        seg_col = jnp.zeros((t, t), jnp.int32)
        segs = [jnp.zeros((t, 1), jnp.int32) for _ in range(self.taps)]
        end = jnp.int32(0)
        for s in range(lens_ref.shape[1]):
            end = end + lens_ref[m, s]
            seg_row = seg_row + jnp.where(row >= end, 1, 0)
            seg_col = seg_col + jnp.where(col >= end, 1, 0)
            segs = [v + jnp.where(token - k >= end, 1, 0) for k, v in enumerate(segs)]
        causal = (row >= col) & (seg_row == seg_col)
        tri = jnp.where(row >= col, 1.0, 0.0).astype(BF16)
        keep = [
            jnp.where((token >= k) & (segs[k] == segs[0]), 1.0, 0.0) for k in range(self.taps)
        ]
        return causal, tri, keep

    def forward(self, u, w, prm, s, masks):
        chan, heads_prm, w_dt = prm
        causal, tri, keep = masks
        t, inner, taps = self.tok, self.inner, self.taps
        rs = lax.rsqrt(jnp.mean(u * u, axis=-1, keepdims=True) + EPS)
        q = u * rs
        normed = (q * chan[6:7, : self.width]).astype(BF16)
        for c in range(0, self.proj, CHUNK):
            s["proj"][:, c : c + CHUNK] = nn(normed, w["in"][:, c : c + CHUNK])
        dtv = nn(normed, w_dt[...]) + heads_prm[0:1, :]
        step = softplus(dtv)
        rate = jnp.exp(heads_prm[1:2, :])
        la = -step * rate
        cum = sum(nn(tri, part) for part in split3(la))
        cum_t = cum.T
        for c in range(0, self.convolved, CHUNK):
            cols = slice(c, c + CHUNK)
            ci = s["proj"][:, inner + c : inner + c + CHUNK]
            pre = chan[taps : taps + 1, cols] + chan[taps - 1 : taps, cols] * ci
            for k in range(1, taps):
                pre = pre + chan[taps - 1 - k : taps - k, cols] * (
                    pltpu.roll(ci, k, 0) * keep[k]
                )
            if "pre" in s:
                s["pre"][:, cols] = pre
            s["co"][:, cols] = pre * sigmoid(pre)
        bm = s["co"][:, inner : inner + self.state].astype(BF16)
        cm = s["co"][:, inner + self.state : inner + 2 * self.state].astype(BF16)
        scores = nt(cm, bm)
        step_hi, step_lo = split2(step)
        for c in range(0, inner, CHUNK):
            cols = slice(c, c + CHUNK)
            spread = nn(step_hi, s["e"][:, cols]) + nn(step_lo, s["e"][:, cols])
            if "stepx" in s:
                s["stepx"][:, cols] = spread
            s["xs"][:, cols] = (s["co"][:, cols] * spread).astype(BF16)
        low_half = lax.broadcasted_iota(jnp.int32, (t, LANES), 1) < self.head_width
        for pair in range(inner // LANES):
            cols = slice(pair * LANES, (pair + 1) * LANES)
            parts = []
            for h in (2 * pair, 2 * pair + 1):
                gap = jnp.where(causal, cum[:, h : h + 1] - cum_t[h : h + 1, :], -1e30)
                decay = jnp.exp(gap)
                if "decay" in s:
                    s["decay"][h] = decay
                parts.append((decay * scores).astype(BF16))
            xs = s["xs"][:, cols].astype(F32)
            blocks = jnp.concatenate(
                [jnp.where(low_half, xs, 0.0).astype(BF16), jnp.where(low_half, 0.0, xs).astype(BF16)],
                axis=0,
            )
            s["ys"][:, cols] = nn(jnp.concatenate(parts, axis=1), blocks)
        total = jnp.zeros((t, 1), F32)
        for c in range(0, inner, CHUNK):
            cols = slice(c, c + CHUNK)
            z = s["proj"][:, cols]
            y = s["ys"][:, cols] + chan[7:8, cols] * s["co"][:, cols]
            gated = y * (z * sigmoid(z))
            s["gated"][:, cols] = gated
            total = total + jnp.sum(gated * gated, axis=-1, keepdims=True)
        r = lax.rsqrt(total * (1.0 / inner) + EPS)
        for c in range(0, inner, CHUNK):
            cols = slice(c, c + CHUNK)
            s["mixed"][:, cols] = (s["gated"][:, cols] * r * chan[5:6, cols]).astype(BF16)
        out = u + nn(s["mixed"][...], w["out"][...])
        return out, dict(
            rs=rs, q=q, normed=normed, dtv=dtv, step=step, rate=rate, la=la,
            bm=bm, cm=cm, scores=scores, r=r, low_half=low_half,
        )

    def backward(self, dres, kept, w, prm, s, masks, small, rows, lanes):
        chan, heads_prm, w_dt = prm
        causal, tri, keep = masks
        t, inner, taps = self.tok, self.inner, self.taps
        dout = dres
        r, low_half = kept["r"], kept["low_half"]
        s["normed_t"][:, lanes] = kept["normed"].astype(F32).T.astype(BF16)
        dot_total = jnp.zeros((t, 1), F32)
        for c in range(0, inner, CHUNK):
            cols = slice(c, c + CHUNK)
            s["mixed_t"][cols, lanes] = s["mixed"][:, cols].astype(F32).T.astype(BF16)
            dm = nt(dout, w["out"][cols, :])
            ghat = s["gated"][:, cols] * r
            prod = dm * ghat
            small[5:6, cols] += jnp.sum(prod, axis=0, keepdims=True)
            dgh = dm * chan[5:6, cols]
            dot_total = dot_total + jnp.sum(dgh * ghat, axis=-1, keepdims=True)
            s["dy"][:, cols] = dgh
        mean_dot = dot_total * (1.0 / inner)
        for c in range(0, inner, CHUNK):
            cols = slice(c, c + CHUNK)
            x = s["co"][:, cols]
            dgated = r * (s["dy"][:, cols] - s["gated"][:, cols] * (r * mean_dot))
            z = s["proj"][:, cols]
            sg = sigmoid(z)
            y = s["ys"][:, cols] + chan[7:8, cols] * x
            dy = dgated * (z * sg)
            s["dproj"][rows, cols] = (dgated * y * (sg * (1.0 + z * (1.0 - sg)))).astype(BF16)
            s["dy"][:, cols] = dy
            small[7:8, cols] += jnp.sum(dy * x, axis=0, keepdims=True)
        ds = jnp.zeros((t, t), F32)
        scores = kept["scores"]
        for pair in range(inner // LANES):
            cols = slice(pair * LANES, (pair + 1) * LANES)
            h = 2 * pair
            dy = s["dy"][:, cols]
            dyb = dy.astype(BF16)
            dyr = dyb.astype(F32)
            xsb = s["xs"][:, cols]
            stacked = jnp.concatenate(
                [jnp.where(low_half, dyr, 0.0).astype(BF16), jnp.where(low_half, 0.0, dyr).astype(BF16)],
                axis=0,
            )
            dw = nt(stacked, xsb)
            decay0, decay1 = s["decay"][h], s["decay"][h + 1]
            ds = ds + dw[:t] * decay0 + dw[t:] * decay1
            weights = jnp.concatenate(
                [(decay0 * scores).astype(BF16), (decay1 * scores).astype(BF16)], axis=0
            )
            dxs = tn(weights, stacked)
            x = s["co"][:, cols]
            s["dco"][:, cols] = dxs * s["stepx"][:, cols] + chan[7:8, cols] * dy
            s["t1"][:, cols] = dyr * s["ys"][:, cols] - dxs * xsb.astype(F32)
            s["t2"][:, cols] = dxs * x
        dcum = sum(nt(part, s["e"][...]) for part in split2(s["t1"][...]))
        dstep = sum(nt(part, s["e"][...]) for part in split2(s["t2"][...]))
        dla = sum(tn(tri, part) for part in split3(dcum))
        dstep = dstep - kept["rate"] * dla
        ddt = dstep * sigmoid(kept["dtv"])
        small[8:9, 0:LANES] += jnp.sum(ddt, axis=0, keepdims=True)
        small[9:10, 0:LANES] += jnp.sum(dla * kept["la"], axis=0, keepdims=True)
        ddtb = ddt.astype(BF16)
        s["ddt"][rows, :] = ddtb
        dsb = ds.astype(BF16)
        s["dco"][:, inner : inner + self.state] = tn(dsb, kept["cm"])
        s["dco"][:, inner + self.state : inner + 2 * self.state] = nn(dsb, kept["bm"])
        for c in range(0, self.convolved, CHUNK):
            cols = slice(c, c + CHUNK)
            ci = s["proj"][:, inner + c : inner + c + CHUNK]
            pre = s["pre"][:, cols]
            sg = sigmoid(pre)
            dpre = s["dco"][:, cols] * (sg * (1.0 + pre * (1.0 - sg)))
            small[taps : taps + 1, cols] += jnp.sum(dpre, axis=0, keepdims=True)
            small[taps - 1 : taps, cols] += jnp.sum(dpre * ci, axis=0, keepdims=True)
            dci = chan[taps - 1 : taps, cols] * dpre
            for k in range(1, taps):
                back = dpre * keep[k]
                small[taps - 1 - k : taps - k, cols] += jnp.sum(
                    back * pltpu.roll(ci, k, 0), axis=0, keepdims=True
                )
                dci = dci + chan[taps - 1 - k : taps - k, cols] * pltpu.roll(back, t - k, 0)
            s["dproj"][rows, inner + c : inner + c + CHUNK] = dci.astype(BF16)
        dnormed = nt(s["dproj"][rows, :], w["in"][...]) + nt(ddtb, w_dt[...])
        q, rs = kept["q"], kept["rs"]
        small[6:7, : self.width] += jnp.sum(dnormed * q, axis=0, keepdims=True)
        dq = dnormed * chan[6:7, : self.width]
        return dres.astype(F32) + rs * (dq - q * jnp.mean(dq * q, axis=-1, keepdims=True))


NAMES = ("e", "proj", "co", "xs", "ys", "gated", "mixed")
BACK_NAMES = ("pre", "decay", "stepx", "dy", "dco", "t1", "t2", "normed_t", "mixed_t", "dproj", "ddt")
SMALL_ROWS = 16
GROUPS = 4
CHUNKS = 2
ORDERED = True
DIRECT = (False, False)


def load_weights(layer, plan, packed, w, sems, me):
    copies = []
    own = layer.width // plan.shards
    for i, (ref, (k, first)) in enumerate(zip(packed, plan.parts)):
        owner, rows = lax.bitwise_xor(me, k), ref.shape[0]

        def place(columns, dst, start, which):
            at = pl.ds(pl.multiple_of(start, 16), rows)
            copies.append(pltpu.make_async_copy(ref.at[:, columns], dst.at[at, :], sems.at[which, i]))

        place(slice(0, layer.proj), w["in"], owner * own + first, 0)
        for r in range(layer.inner // layer.width):
            columns = slice(layer.proj + r * layer.width, layer.proj + (r + 1) * layer.width)
            place(columns, w["out"], owner * (layer.inner // plan.shards) + r * own + first, 1 + r)
    for copy in copies:
        copy.start()
    for copy in copies:
        copy.wait()


def fill_spread(layer, ref):
    head = lax.broadcasted_iota(jnp.int32, ref.shape, 0) * layer.head_width
    lane = lax.broadcasted_iota(jnp.int32, ref.shape, 1)
    ref[...] = jnp.where((lane >= head) & (lane < head + layer.head_width), 1.0, 0.0).astype(BF16)


class Plan(NamedTuple):
    shards: int
    parts: tuple


def forward_kernel(layer, micro, plan, section, *refs):
    lens, u_ref, chan, heads_prm, w_dt = refs[:5]
    count = len(plan.parts)
    packed = refs[5 : 5 + count]
    y_ref, w_in, w_out, *scr, sems = refs[5 + count :]
    s = dict(zip(NAMES, scr))
    w = {"in": w_in, "out": w_out}

    @pl.when(lax.axis_index("section") == section)
    def _():
        load_weights(layer, plan, packed, w, sems, lax.axis_index("shard"))
        fill_spread(layer, s["e"])

        @pl.loop(0, micro)
        def _(m):
            rows = pl.ds(pl.multiple_of(m * layer.tok, layer.tok), layer.tok)
            out, _ = layer.forward(
                u_ref[rows, :].astype(F32), w, (chan, heads_prm, w_dt), s, layer.masks(lens, m)
            )
            y_ref[rows, :] = out.astype(BF16)


def pack_small(layer, n, j, small, ref):
    row = lax.broadcasted_iota(jnp.int32, (SMALL_ROWS, layer.convolved), 0)
    all_rows = small[...]

    def from_owner(v, own):
        return pltpu.roll(v, (layer.convolved - j * own) % layer.convolved, 1) if j else v

    mine = from_owner(all_rows, layer.convolved // n)
    mine = jnp.where(row == 5, from_owner(all_rows, layer.inner // n), mine)
    mine = jnp.where(row == 6, from_owner(all_rows, layer.width // n), mine)
    mine = jnp.where(row >= 7, from_owner(all_rows, layer.heads // n), mine)
    for g in range(GROUPS):
        ref[g * SMALL_ROWS : (g + 1) * SMALL_ROWS, LANES:CHUNK] = mine[
            :, g * LANES : (g + 1) * LANES
        ].astype(BF16)


def both_kernel(layer, micro, plan, section, *refs):
    n = plan.shards
    lens, u_ref, chan, heads_prm, w_dt, dres_ref = refs[:6]
    count = len(plan.parts)
    packed = refs[6 : 6 + count]
    y_ref, din_ref, dlow_ref = refs[6 + count : 9 + count]
    ends = 9 + count + 4 * CHUNKS
    outs = refs[9 + count : ends]
    w_in, w_out, *scr, small, gbuf, sems, gsems = refs[ends:]
    s = dict(zip(NAMES + BACK_NAMES, scr))
    w = {"in": w_in, "out": w_out}
    group = gbuf.shape[1] // (2 * CHUNKS)
    targets = []
    for c in range(CHUNKS):
        keep_a, send_a, keep_b, send_b = outs[4 * c : 4 * c + 4]
        targets.append((keep_a.at[0], send_a.at[0], keep_a.at[1], send_a.at[1]))
        targets.append((keep_b.at[0], keep_b.at[1], send_b.at[0], send_b.at[1]))

    @pl.when(lax.axis_index("section") == section)
    def _():
        me = lax.axis_index("shard")
        load_weights(layer, plan, packed, w, sems, me)
        fill_spread(layer, s["e"])
        small[...] = jnp.zeros(small.shape, F32)

        @pl.loop(0, micro)
        def _(m):
            start = pl.multiple_of(m * layer.tok, layer.tok)
            rows = pl.ds(start, layer.tok)
            prm = (chan, heads_prm, w_dt)
            masks = layer.masks(lens, m)
            out, kept = layer.forward(u_ref[rows, :].astype(F32), w, prm, s, masks)
            y_ref[rows, :] = out.astype(BF16)
            din = layer.backward(dres_ref[rows, :], kept, w, prm, s, masks, small, rows, rows)
            din_ref[rows, :] = din
            dlow_ref[rows, :] = din.astype(BF16)

        def send_off(which, j):
            for k in range(n):

                @pl.when(lax.bitwise_xor(me, k) == j)
                def _(k=k):
                    pltpu.make_async_copy(
                        gbuf.at[j, which * group : (which + 1) * group], targets[which][k], gsems.at[which, k]
                    ).start()

        in_rows, in_blocks, out_blocks = layer.width // n, layer.proj // CHUNK, layer.width // CHUNK

        def in_block(j, b):
            part = slice(j * in_rows, (j + 1) * in_rows)
            gbuf[j, b] = nn(
                s["normed_t"][part, :], s["dproj"][:, b * CHUNK : (b + 1) * CHUNK]
            ).astype(BF16)

        skip = sum(nt(part, s["e"][...]) for part in split2(small[7:8, : layer.inner]))
        small[7:8, :LANES] = skip
        def out_block(j, b):
            r, c = divmod(b, out_blocks)
            first = j * (layer.inner // n) + r * in_rows
            gbuf[j, in_blocks + b] = nn(
                s["mixed_t"][first : first + in_rows, :], dres_ref[:, c * CHUNK : (c + 1) * CHUNK]
            ).astype(BF16)

        def last_block(j):
            last = gbuf.at[j, 2 * CHUNKS * group - 1]
            last[...] = jnp.zeros(last.shape, BF16)
            last[:, :LANES] = nn(
                s["normed_t"][j * in_rows : (j + 1) * in_rows, :], s["ddt"][...]
            ).astype(BF16)
            pack_small(layer, n, j, small, last)

        matrices = in_blocks + layer.inner // layer.width * out_blocks
        for which in range(2 * CHUNKS):
            for j in range(n):
                for b in range(which * group, (which + 1) * group):
                    if b < in_blocks:
                        in_block(j, b)
                    elif b < matrices:
                        out_block(j, b - in_blocks)
                    elif b == 2 * CHUNKS * group - 1:
                        last_block(j)
                    else:
                        gbuf[j, b] = jnp.zeros(gbuf.shape[2:], BF16)
                send_off(which, j)
        for which in range(2 * CHUNKS):
            for k in range(n):
                pltpu.make_async_copy(
                    gbuf.at[k, which * group : (which + 1) * group], targets[which][k], gsems.at[which, k]
                ).wait()


VMEM = pl.BlockSpec(memory_space=pltpu.VMEM)
ANY = pl.BlockSpec(memory_space=pl.ANY)


def call_layer(layer, micro, plan, section, backward, lens, u, prm, pieces, dres=None):
    n = plan.shards
    tokens = micro * layer.tok
    smem = pl.BlockSpec(memory_space=pltpu.SMEM)
    scratch = layer.scratch(backward, micro)
    y = jax.ShapeDtypeStruct((tokens, layer.width), BF16)
    work = 2 * tokens * layer.width * (layer.proj + layer.inner)
    cost = pl.CostEstimate(
        flops=work * (4 if backward else 1),
        bytes_accessed=8_000_000 * (2 if backward else 1),
        transcendentals=tokens * layer.tok * layer.heads,
    )
    params = pltpu.CompilerParams(vmem_limit_bytes=VMEM_LIMIT)
    load_sems = pltpu.SemaphoreType.DMA((1 + layer.inner // layer.width, len(plan.parts)))
    if not backward:
        return pl.pallas_call(
            functools.partial(forward_kernel, layer, micro, plan, section),
            out_shape=y,
            in_specs=[smem] + [VMEM] * 4 + [ANY] * len(pieces),
            out_specs=VMEM,
            scratch_shapes=scratch + [load_sems],
            compiler_params=params,
            cost_estimate=cost,
            name="layer_forward",
        )(lens, u, *prm, *pieces)
    blocks = layer.blocks(n)
    packed = jax.ShapeDtypeStruct((2, blocks // (2 * CHUNKS), layer.width // n, CHUNK), BF16)
    return pl.pallas_call(
        functools.partial(both_kernel, layer, micro, plan, section),
        out_shape=[y, jax.ShapeDtypeStruct((tokens, layer.width), F32), y] + [packed] * (4 * CHUNKS),
        in_specs=[smem] + [VMEM] * 5 + [ANY] * len(pieces),
        out_specs=[VMEM] * 3 + [ANY] * (4 * CHUNKS),
        scratch_shapes=scratch
        + [
            pltpu.VMEM((SMALL_ROWS, layer.convolved), F32),
            pltpu.VMEM((n, blocks, layer.width // n, CHUNK), BF16),
            load_sems,
            pltpu.SemaphoreType.DMA((2 * CHUNKS, n)),
        ],
        compiler_params=params,
        cost_estimate=cost,
        name="layer_both",
    )(lens, u, *prm, dres, *pieces)


def copy_all(pairs, sems):
    copies = [pltpu.make_async_copy(src, dst, sems.at[i]) for i, (src, dst) in enumerate(pairs)]
    for copy in copies:
        copy.start()
    for copy in copies:
        copy.wait()


def pack_kernel(w_in, w_out, top, bottom, sems):
    proj, rows, width = w_in.shape[1], w_in.shape[0], w_out.shape[1]
    half = rows // 2
    pairs = []
    for i, out in enumerate((top, bottom)):
        pairs.append((w_in.at[i * half : (i + 1) * half, :], out.at[:, :proj]))
        for r in range(w_out.shape[0] // rows):
            columns = slice(proj + r * width, proj + (r + 1) * width)
            first = r * rows + i * half
            pairs.append((w_out.at[first : first + half, :], out.at[:, columns]))
    copy_all(pairs, sems)


def pack(w_in, w_out):
    groups = w_out.shape[0] // w_in.shape[0]
    half = jax.ShapeDtypeStruct((w_in.shape[0] // 2, w_in.shape[1] + groups * w_out.shape[1]), BF16)
    return pl.pallas_call(
        pack_kernel,
        out_shape=[half, half],
        in_specs=[ANY, ANY],
        out_specs=[VMEM, VMEM],
        scratch_shapes=[pltpu.SemaphoreType.DMA((2 * (1 + groups),))],
        cost_estimate=pl.CostEstimate(flops=0, bytes_accessed=4_000_000, transcendentals=0),
        name="pack",
    )(w_in, w_out)


def hold_kernel(section, count, waits, *refs):
    values, outs = refs[:count], refs[count + waits : 2 * count + waits]
    bufs, sems = refs[2 * count + waits : -1], refs[-1]

    def move():
        copy_all(list(zip(values, bufs)), sems)
        copy_all(list(zip(bufs, outs)), sems)

    if section is None:
        move()
    else:
        pl.when(lax.axis_index("section") == section)(move)


def hold(values, tokens, section=None):
    return pl.pallas_call(
        functools.partial(hold_kernel, section, len(values), len(tokens)),
        out_shape=[jax.ShapeDtypeStruct(v.shape, v.dtype) for v in values],
        in_specs=[ANY] * (len(values) + len(tokens)),
        out_specs=[ANY] * len(values),
        scratch_shapes=[pltpu.VMEM(v.shape, v.dtype) for v in values]
        + [pltpu.SemaphoreType.DMA((len(values),))],
        cost_estimate=pl.CostEstimate(flops=0, bytes_accessed=4_000_000, transcendentals=0),
        name="hold",
    )(*values, *tokens)


def pass_on_kernel(section, keep_a, got_a, keep_b, got_b, *refs):
    out_a, out_b, buf, sems = refs[-4:]

    @pl.when(lax.axis_index("section") == section)
    def _():
        sources = (keep_a, got_a, keep_b, got_b)
        copy_all([(ref.at[1], buf.at[i]) for i, ref in enumerate(sources)], sems)
        for i in range(buf.shape[1]):
            out_a[i] = (buf[0, i].astype(F32) + buf[1, i].astype(F32)).astype(BF16)
            out_b[i] = (buf[2, i].astype(F32) + buf[3, i].astype(F32)).astype(BF16)


def sum_to_pass_on(section, terms, tokens):
    shape = terms[0].shape[1:]
    return pl.pallas_call(
        functools.partial(pass_on_kernel, section),
        out_shape=[jax.ShapeDtypeStruct(shape, BF16)] * 2,
        in_specs=[ANY] * (4 + len(tokens)),
        out_specs=[VMEM] * 2,
        scratch_shapes=[pltpu.VMEM((4,) + shape, BF16), pltpu.SemaphoreType.DMA((4,))],
        cost_estimate=pl.CostEstimate(flops=1_000_000, bytes_accessed=3_000_000, transcendentals=0),
        name="sum_to_pass_on",
    )(*terms, *tokens)


def dp_part(parts, k):
    return lax.bitwise_xor(lax.axis_index("dp") & (parts - 1), k)


def cut_kernel(section, parts, keep_a, got_a, last_a, keep_b, got_b, last_b, *refs):
    outs, (buf, sems) = refs[:parts], refs[parts:]

    @pl.when(lax.axis_index("section") == section)
    def _():
        sources = (keep_a.at[0], got_a.at[0], last_a, keep_b.at[0], got_b.at[0], last_b)
        copies = [
            pltpu.make_async_copy(ref, buf.at[i], sems.at[i]) for i, ref in enumerate(sources)
        ]
        for copy in copies:
            copy.start()
        half, rows = buf.shape[1], buf.shape[2] // parts
        for h in range(2):
            for copy in copies[3 * h : 3 * h + 3]:
                copy.wait()
            for k in range(parts):
                part = pl.ds(pl.multiple_of(dp_part(parts, k) * rows, rows), rows)
                for i in range(half):
                    total = sum(buf[3 * h + t, i, part, :].astype(F32) for t in range(3))
                    outs[k][h * half + i] = total.astype(BF16)


def cut_for_dp(section, parts, operands):
    _, half, rows, columns = operands[0].shape
    return pl.pallas_call(
        functools.partial(cut_kernel, section, parts),
        out_shape=[jax.ShapeDtypeStruct((2 * half, rows // parts, columns), BF16)] * parts,
        in_specs=[ANY] * 6,
        out_specs=[VMEM] * parts,
        scratch_shapes=[
            pltpu.VMEM((6, half, rows, columns), BF16),
            pltpu.SemaphoreType.DMA((6,)),
        ],
        compiler_params=pltpu.CompilerParams(vmem_limit_bytes=VMEM_LIMIT),
        cost_estimate=pl.CostEstimate(flops=5_000_000, bytes_accessed=8_000_000, transcendentals=0),
        name="cut_for_dp",
    )(*operands)


def unpack_kernel(layer, n, counts, *refs):
    sets, at = [], 0
    for count in counts:
        sets.append([refs[at + c * count : at + (c + 1) * count] for c in range(CHUNKS)])
        at += CHUNKS * count
    norm, w_in, w_dt, conv_w, conv_b, dt_bias, a_log, skip, inner, w_out, buf, sems = refs[at:]

    for which, (count, chunks) in enumerate(zip(counts, sets)):

        @pl.when(lax.axis_index("section") == which)
        def _(count=count, chunks=chunks):
            copies = []
            for c in range(CHUNKS):
                for k in range(count):
                    ref = chunks[c][k]
                    blocks, rows = ref.shape[:2]
                    start = pl.multiple_of(dp_part(count, k) * rows, rows)
                    dst = buf.at[c * blocks : (c + 1) * blocks, pl.ds(start, rows), :]
                    copies.append(pltpu.make_async_copy(ref, dst, sems.at[c, k]))
            for copy in copies:
                copy.start()
            for copy in copies:
                copy.wait()

    in_blocks, out_blocks = layer.proj // CHUNK, layer.width // CHUNK
    in_rows = buf.shape[1]
    for b in range(in_blocks):
        w_in[:, b * CHUNK : (b + 1) * CHUNK] = buf[b].astype(F32)
    for r in range(layer.inner // layer.width):
        for c in range(out_blocks):
            w_out[r * in_rows : (r + 1) * in_rows, c * CHUNK : (c + 1) * CHUNK] = buf[
                in_blocks + r * out_blocks + c
            ].astype(F32)
    last = buf.shape[0] - 1
    w_dt[...] = buf[last, :, :LANES].astype(F32).T[: layer.heads, :]

    def channels(row, ref, row_count=1):
        count = ref.shape[1]
        for g in range(-(-count // LANES)):
            lanes = min(LANES, count - g * LANES)
            group = buf[last, g * SMALL_ROWS : (g + 1) * SMALL_ROWS, LANES:CHUNK].astype(F32)
            ref[:, g * LANES : g * LANES + lanes] = group[row : row + row_count, :lanes]

    channels(0, conv_w, layer.taps)
    channels(layer.taps, conv_b)
    channels(5, inner)
    channels(6, norm)
    channels(7, skip)
    channels(8, dt_bias)
    channels(9, a_log)


def unpack(layer, n, first, second):
    counts = (len(first[0]), len(second[0]))
    operands = [part for chunks in (first, second) for chunk in chunks for part in chunk]
    shapes = (
        (1, layer.width // n), (layer.width // n, layer.proj), (layer.heads, layer.width // n),
        (layer.taps, layer.convolved // n), (1, layer.convolved // n), (1, layer.heads // n),
        (1, layer.heads // n), (1, layer.heads // n), (1, layer.inner // n), (layer.inner // n, layer.width),
    )
    return pl.pallas_call(
        functools.partial(unpack_kernel, layer, n, counts),
        out_shape=[jax.ShapeDtypeStruct(shape, F32) for shape in shapes],
        in_specs=[ANY] * len(operands),
        out_specs=[VMEM] * len(shapes),
        scratch_shapes=[
            pltpu.VMEM((layer.blocks(n), layer.width // n, CHUNK), BF16),
            pltpu.SemaphoreType.DMA((CHUNKS, max(counts))),
        ],
        compiler_params=pltpu.CompilerParams(vmem_limit_bytes=VMEM_LIMIT),
        cost_estimate=pl.CostEstimate(flops=0, bytes_accessed=6_000_000, transcendentals=0),
        name="unpack",
    )(*operands)


def exchange(block, axis, distance, section=None):
    size = lax.axis_size(axis)
    if section is None:
        return lax.ppermute(block, axis, [(i, i ^ distance) for i in range(size)])
    base = section * size
    route = [(base + i, base + (i ^ distance)) for i in range(size)]
    return lax.ppermute(block, ("section", axis), route)


def wide_sum(*parts):
    return sum(part.astype(F32) for part in parts)


X_WAY, Y_WAY, BOTH_WAYS = 1, 2, 3


def gather(halves, section):
    top, bottom = halves
    x_top = exchange(top, "shard", X_WAY, section)
    y_bottom = exchange(bottom, "shard", Y_WAY, section)
    x_bottom = exchange(bottom, "shard", X_WAY, section)
    y_top = exchange(top, "shard", Y_WAY, section)
    far_top = exchange(x_top, "shard", Y_WAY, section)
    far_bottom = exchange(y_bottom, "shard", X_WAY, section)
    return x_top, x_bottom, y_top, y_bottom, far_top, far_bottom


def sum_over_shard(packed, section, tokens):
    keep_a, send_a, keep_b, send_b = packed
    got_a = exchange(send_a, "shard", X_WAY, section)
    got_b = exchange(send_b, "shard", Y_WAY, section)
    far_a, far_b = sum_to_pass_on(section, (keep_a, got_a, keep_b, got_b), tokens)
    last_a = exchange(far_a, "shard", Y_WAY, section)
    last_b = exchange(far_b, "shard", X_WAY, section)
    return keep_a, got_a, last_a, keep_b, got_b, last_b


def sum_layer(packed, section):
    done, tokens = [], ()
    for c in range(CHUNKS):
        terms = sum_over_shard(packed[4 * c : 4 * c + 4], section, tokens)
        tokens = (terms[2], terms[5]) if ORDERED else ()
        done.append(sum_over_dp(terms, section, DIRECT[section]))
    return done


def sum_over_dp(terms, section, direct):
    size = lax.axis_size("dp")
    if size != 4:
        [total] = cut_for_dp(section, 1, terms)
        return [lax.psum(total, "dp")]
    if direct:
        parts = cut_for_dp(section, 4, terms)
        got = [exchange(parts[k], "dp", k, section) for k in range(1, 4)]
        done = wide_sum(parts[0], *got).astype(BF16)
        return [done] + [exchange(done, "dp", k, section) for k in range(1, 4)]
    own, other = cut_for_dp(section, 2, terms)
    pair = wide_sum(own, exchange(other, "dp", 1, section)).astype(BF16)
    done = wide_sum(pair, exchange(pair, "dp", 2, section)).astype(BF16)
    return [done, exchange(done, "dp", 1, section)]


def in_order(by_distance, me):
    a, b, c, d = by_distance
    odd, high = (me & 1) != 0, (me & 2) != 0
    a, b = jnp.where(odd, b, a), jnp.where(odd, a, b)
    c, d = jnp.where(odd, d, c), jnp.where(odd, c, d)
    return [jnp.where(high, p, q) for p, q in ((c, a), (d, b), (a, c), (b, d))]


def body(
    tokens_in, seq_lengths, out_grad, norm_gain, w_in, w_dt, conv_w, conv_b,
    dt_bias, a_log, d_skip, inner_gain, w_out,
):
    is_first = lax.axis_index("section") == 0
    shard_pos = lax.axis_index("shard")
    n = lax.axis_size("shard")
    micro, tok, width = tokens_in.shape
    own_heads = dt_bias.shape[1]
    heads, taps = own_heads * n, conv_w.shape[1]
    inner, convolved = inner_gain.shape[1] * n, conv_b.shape[1] * n
    layer = Layer(tok, width, inner, convolved, heads, taps)

    own_conv, own_inner, own_width = conv_b.shape[1], inner_gain.shape[1], norm_gain.shape[1]
    flat = jnp.concatenate(
        [v.reshape(-1) for v in (conv_w, conv_b, inner_gain, norm_gain, dt_bias, a_log, d_skip, w_dt)]
    )
    packed = -(-flat.shape[0] // 2048) * 2048
    flat = jnp.pad(flat, (0, packed - flat.shape[0])).reshape(-1, LANES)
    def parameters(flats):
        everyone = jnp.stack(in_order(flats, shard_pos)).reshape(n, packed)
        at = [0]

        def take(count):
            at[0] += count
            return everyone[:, at[0] - count : at[0]]

        conv_w_all = take(taps * own_conv).reshape(n, taps, own_conv).transpose(1, 0, 2).reshape(taps, convolved)
        conv_b_all = take(own_conv).reshape(1, convolved)
        inner_all = take(own_inner).reshape(1, inner)
        norm_all = take(own_width).reshape(1, width)
        dt_bias_all = take(own_heads).reshape(1, heads)
        a_log_all = take(own_heads).reshape(1, heads)
        d_skip_all = take(own_heads).reshape(1, heads)
        w_dt_all = jnp.pad(take(own_width * heads).reshape(width, heads), ((0, 0), (0, LANES - heads)))

        def padded(row):
            return jnp.pad(row, ((0, 0), (0, convolved - row.shape[1])))

        skip_all = jnp.repeat(d_skip_all, inner // heads, axis=1)
        chan = jnp.concatenate(
            [conv_w_all, conv_b_all, padded(inner_all), padded(norm_all), padded(skip_all)], axis=0
        ).astype(F32)
        heads_prm = jnp.pad(
            jnp.concatenate([dt_bias_all, a_log_all], axis=0), ((0, 6), (0, LANES - heads))
        ).astype(F32)
        return chan, heads_prm, w_dt_all

    half = own_width // 2
    plan = Plan(n, tuple((k, first) for k in (0, X_WAY, Y_WAY, BOTH_WAYS) for first in (0, half)))
    own_w = tuple(pack(w_in[0], w_out[0]))
    near = gather(own_w, 0)
    first_w = own_w + near
    [flat] = hold((flat,), near[:1])
    flats = [flat] + [exchange(flat, "shard", k) for k in (X_WAY, Y_WAY, BOTH_WAYS)]
    token = lax.ppermute(near[1][:16, :LANES], "section", [(0, 1)])
    second_w = own_w + gather(hold(own_w, (token,), 1), 1)
    prm = parameters(hold(flats, near[1:3]))

    lens = seq_lengths[:, 0, :]
    tokens = tokens_in.reshape(micro * tok, width)
    cotangent = out_grad.reshape(micro * tok, width)
    hidden = call_layer(layer, micro, plan, 0, False, lens, tokens, prm, first_w)
    arrived = lax.ppermute(hidden, "section", [(0, 1)])
    final, second_in_grad, second_low, *second_g = call_layer(
        layer, micro, plan, 1, True, lens, arrived, prm, second_w, dres=cotangent
    )
    back = lax.ppermute(second_low, "section", [(1, 0)])
    _, first_in_grad, _, *first_g = call_layer(
        layer, micro, plan, 0, True, lens, tokens, prm, first_w, dres=back
    )
    second_done = sum_layer(second_g, 1)
    first_done = sum_layer(first_g, 0)
    g_norm, g_w_in, g_w_dt, g_conv_w, g_conv_b, g_dt_bias, g_a_log, g_d_skip, g_inner, g_w_out = unpack(
        layer, n, first_done, second_done
    )

    shape = (1, micro, tok, width)
    section_out = jnp.where(is_first, hidden, final).reshape(shape)
    section_in_grad = jnp.where(is_first, first_in_grad, second_in_grad).reshape(shape)
    return (
        section_out, section_in_grad, g_norm, g_w_in[None], g_w_dt.T[None], g_conv_w[None], g_conv_b,
        g_dt_bias, g_a_log, g_d_skip, g_inner, g_w_out[None],
    )


def solution(mesh):
    spread = P(None, ("dp", "shard"), None)
    flat, tall, conv = P("section", "shard"), P("section", "shard", None), P("section", None, "shard")
    outer = P("section", None, ("dp", "shard"), None)
    return jax.shard_map(
        body,
        mesh=mesh,
        in_specs=(spread, spread, spread, flat, tall, tall, conv, flat, flat, flat, flat, flat, tall),
        out_specs=(outer, outer, flat, tall, tall, conv, flat, flat, flat, flat, flat, tall),
        check_vma=False,
    )
```

```python
import functools
from typing import NamedTuple

import jax
import jax.numpy as jnp
from jax import lax
from jax.experimental import pallas as pl
from jax.experimental.pallas import tpu as pltpu
from jax.sharding import PartitionSpec as P

EPS = 1e-05
F32 = jnp.float32
BF16 = jnp.bfloat16
LANES = 128
CHUNK = 256
VMEM_LIMIT = 56 * 2**20


def nn(a, b):
    return jnp.dot(a, b, preferred_element_type=F32)


def nt(a, b):
    return lax.dot_general(a, b, (((1,), (1,)), ((), ())), preferred_element_type=F32)


def tn(a, b):
    return lax.dot_general(a, b, (((0,), (0,)), ((), ())), preferred_element_type=F32)


def split2(v):
    hi = v.astype(BF16)
    return hi, (v - hi.astype(F32)).astype(BF16)


def split3(v):
    hi, rest = v.astype(BF16), None
    rest = v - hi.astype(F32)
    mid = rest.astype(BF16)
    return hi, mid, (rest - mid.astype(F32)).astype(BF16)


def softplus(v):
    return jnp.maximum(v, 0.0) + jnp.log1p(jnp.exp(-jnp.abs(v)))


def sigmoid(v):
    return 0.5 + 0.5 * jnp.tanh(0.5 * v)


class Layer:
    def __init__(self, tok, width, inner, convolved, heads, taps):
        self.tok, self.width, self.inner, self.convolved = tok, width, inner, convolved
        self.heads, self.taps = heads, taps
        self.head_width = inner // heads
        self.state = (convolved - inner) // 2
        self.proj = inner + convolved

    def scratch(self, backward, micro):
        t, d, i, c = self.tok, self.width, self.inner, self.convolved
        shapes = [
            pltpu.VMEM((d, self.proj), BF16),
            pltpu.VMEM((i, d), BF16),
            pltpu.VMEM((LANES, i), BF16),
            pltpu.VMEM((micro * t, self.proj), F32),
            pltpu.VMEM((t, c), F32),
            pltpu.VMEM((t, i), BF16),
            pltpu.VMEM((t, i), F32),
            pltpu.VMEM((t, i), F32),
            pltpu.VMEM((micro * t, i), BF16),
            pltpu.VMEM((micro * t, d), BF16),
            pltpu.VMEM((micro * t, LANES), F32),
        ]
        if backward:
            shapes += [
                pltpu.VMEM((t, c), F32),
                pltpu.VMEM((self.heads, t, t), F32),
                pltpu.VMEM((t, i), F32),
                pltpu.VMEM((micro * t, i), F32),
                pltpu.VMEM((t, c), F32),
                pltpu.VMEM((t, i), F32),
                pltpu.VMEM((t, i), F32),
                pltpu.VMEM((d, micro * t), BF16),
                pltpu.VMEM((i, micro * t), BF16),
                pltpu.VMEM((micro * t, self.proj), BF16),
                pltpu.VMEM((micro * t, LANES), BF16),
            ]
        return shapes

    def blocks(self, n):
        matrices = (self.width // n * self.proj + self.inner // n * self.width) // (self.width // n * CHUNK)
        return -(-(matrices + 1) // (2 * CHUNKS)) * 2 * CHUNKS

    def masks(self, lens_ref, m):
        t = self.tok
        row = lax.broadcasted_iota(jnp.int32, (t, t), 0)
        col = lax.broadcasted_iota(jnp.int32, (t, t), 1)
        token = lax.broadcasted_iota(jnp.int32, (t, 1), 0)
        seg_row = jnp.zeros((t, t), jnp.int32)
        seg_col = jnp.zeros((t, t), jnp.int32)
        segs = [jnp.zeros((t, 1), jnp.int32) for _ in range(self.taps)]
        end = jnp.int32(0)
        for s in range(lens_ref.shape[1]):
            end = end + lens_ref[m, s]
            seg_row = seg_row + jnp.where(row >= end, 1, 0)
            seg_col = seg_col + jnp.where(col >= end, 1, 0)
            segs = [v + jnp.where(token - k >= end, 1, 0) for k, v in enumerate(segs)]
        causal = (row >= col) & (seg_row == seg_col)
        tri = jnp.where(row >= col, 1.0, 0.0).astype(BF16)
        keep = [
            jnp.where((token >= k) & (segs[k] == segs[0]), 1.0, 0.0) for k in range(self.taps)
        ]
        return causal, tri, keep

    def normalize(self, u_ref, prm, s):
        u = u_ref[...].astype(F32)
        rs = lax.rsqrt(jnp.mean(u * u, axis=-1, keepdims=True) + EPS)
        s["normed"][...] = (u * rs * prm[0][6:7, : self.width]).astype(BF16)

    def project(self, w, prm, s):
        for c in range(0, self.proj, CHUNK):
            s["proj"][:, c : c + CHUNK] = nn(s["normed"][...], w["in"][:, c : c + CHUNK])
        s["dt"][...] = nn(s["normed"][...], prm[2][...])

    def forward(self, prm, s, masks, rows):
        chan, heads_prm, _ = prm
        causal, tri, keep = masks
        t, inner, taps = self.tok, self.inner, self.taps
        dtv = s["dt"][rows, :] + heads_prm[0:1, :]
        step = softplus(dtv)
        rate = jnp.exp(heads_prm[1:2, :])
        la = -step * rate
        cum = sum(nn(tri, part) for part in split3(la))
        cum_t = cum.T
        for c in range(0, self.convolved, CHUNK):
            cols = slice(c, c + CHUNK)
            ci = s["proj"][rows, inner + c : inner + c + CHUNK]
            pre = chan[taps : taps + 1, cols] + chan[taps - 1 : taps, cols] * ci
            for k in range(1, taps):
                pre = pre + chan[taps - 1 - k : taps - k, cols] * (
                    pltpu.roll(ci, k, 0) * keep[k]
                )
            if "pre" in s:
                s["pre"][:, cols] = pre
            s["co"][:, cols] = pre * sigmoid(pre)
        bm = s["co"][:, inner : inner + self.state].astype(BF16)
        cm = s["co"][:, inner + self.state : inner + 2 * self.state].astype(BF16)
        scores = nt(cm, bm)
        step_hi, step_lo = split2(step)
        for c in range(0, inner, CHUNK):
            cols = slice(c, c + CHUNK)
            spread = nn(step_hi, s["e"][:, cols]) + nn(step_lo, s["e"][:, cols])
            if "stepx" in s:
                s["stepx"][:, cols] = spread
            s["xs"][:, cols] = (s["co"][:, cols] * spread).astype(BF16)
        low_half = lax.broadcasted_iota(jnp.int32, (t, LANES), 1) < self.head_width
        for pair in range(inner // LANES):
            cols = slice(pair * LANES, (pair + 1) * LANES)
            parts = []
            for h in (2 * pair, 2 * pair + 1):
                gap = jnp.where(causal, cum[:, h : h + 1] - cum_t[h : h + 1, :], -1e30)
                decay = jnp.exp(gap)
                if "decay" in s:
                    s["decay"][h] = decay
                parts.append((decay * scores).astype(BF16))
            xs = s["xs"][:, cols].astype(F32)
            blocks = jnp.concatenate(
                [jnp.where(low_half, xs, 0.0).astype(BF16), jnp.where(low_half, 0.0, xs).astype(BF16)],
                axis=0,
            )
            s["ys"][:, cols] = nn(jnp.concatenate(parts, axis=1), blocks)
        total = jnp.zeros((t, 1), F32)
        for c in range(0, inner, CHUNK):
            cols = slice(c, c + CHUNK)
            z = s["proj"][rows, cols]
            y = s["ys"][:, cols] + chan[7:8, cols] * s["co"][:, cols]
            gated = y * (z * sigmoid(z))
            s["gated"][:, cols] = gated
            total = total + jnp.sum(gated * gated, axis=-1, keepdims=True)
        r = lax.rsqrt(total * (1.0 / inner) + EPS)
        for c in range(0, inner, CHUNK):
            cols = slice(c, c + CHUNK)
            s["mixed"][rows, cols] = (s["gated"][:, cols] * r * chan[5:6, cols]).astype(BF16)
        return dict(
            dtv=dtv, step=step, rate=rate, la=la, bm=bm, cm=cm, scores=scores, r=r, low_half=low_half
        )

    def backward(self, kept, prm, s, masks, small, rows):
        chan = prm[0]
        causal, tri, keep = masks
        t, inner, taps = self.tok, self.inner, self.taps
        r, low_half = kept["r"], kept["low_half"]
        dot_total = jnp.zeros((t, 1), F32)
        for c in range(0, inner, CHUNK):
            cols = slice(c, c + CHUNK)
            dm = s["dy"][rows, cols]
            ghat = s["gated"][:, cols] * r
            prod = dm * ghat
            small[5:6, cols] += jnp.sum(prod, axis=0, keepdims=True)
            dgh = dm * chan[5:6, cols]
            dot_total = dot_total + jnp.sum(dgh * ghat, axis=-1, keepdims=True)
            s["dy"][rows, cols] = dgh
        mean_dot = dot_total * (1.0 / inner)
        for c in range(0, inner, CHUNK):
            cols = slice(c, c + CHUNK)
            x = s["co"][:, cols]
            dgated = r * (s["dy"][rows, cols] - s["gated"][:, cols] * (r * mean_dot))
            z = s["proj"][rows, cols]
            sg = sigmoid(z)
            y = s["ys"][:, cols] + chan[7:8, cols] * x
            dy = dgated * (z * sg)
            s["dproj"][rows, cols] = (dgated * y * (sg * (1.0 + z * (1.0 - sg)))).astype(BF16)
            s["dy"][rows, cols] = dy
            small[7:8, cols] += jnp.sum(dy * x, axis=0, keepdims=True)
        ds = jnp.zeros((t, t), F32)
        scores = kept["scores"]
        for pair in range(inner // LANES):
            cols = slice(pair * LANES, (pair + 1) * LANES)
            h = 2 * pair
            dy = s["dy"][rows, cols]
            dyb = dy.astype(BF16)
            dyr = dyb.astype(F32)
            xsb = s["xs"][:, cols]
            stacked = jnp.concatenate(
                [jnp.where(low_half, dyr, 0.0).astype(BF16), jnp.where(low_half, 0.0, dyr).astype(BF16)],
                axis=0,
            )
            dw = nt(stacked, xsb)
            decay0, decay1 = s["decay"][h], s["decay"][h + 1]
            ds = ds + dw[:t] * decay0 + dw[t:] * decay1
            weights = jnp.concatenate(
                [(decay0 * scores).astype(BF16), (decay1 * scores).astype(BF16)], axis=0
            )
            dxs = tn(weights, stacked)
            x = s["co"][:, cols]
            s["dco"][:, cols] = dxs * s["stepx"][:, cols] + chan[7:8, cols] * dy
            s["t1"][:, cols] = dyr * s["ys"][:, cols] - dxs * xsb.astype(F32)
            s["t2"][:, cols] = dxs * x
        dcum = sum(nt(part, s["e"][...]) for part in split2(s["t1"][...]))
        dstep = sum(nt(part, s["e"][...]) for part in split2(s["t2"][...]))
        dla = sum(tn(tri, part) for part in split3(dcum))
        dstep = dstep - kept["rate"] * dla
        ddt = dstep * sigmoid(kept["dtv"])
        small[8:9, 0:LANES] += jnp.sum(ddt, axis=0, keepdims=True)
        small[9:10, 0:LANES] += jnp.sum(dla * kept["la"], axis=0, keepdims=True)
        ddtb = ddt.astype(BF16)
        s["ddt"][rows, :] = ddtb
        dsb = ds.astype(BF16)
        s["dco"][:, inner : inner + self.state] = tn(dsb, kept["cm"])
        s["dco"][:, inner + self.state : inner + 2 * self.state] = nn(dsb, kept["bm"])
        for c in range(0, self.convolved, CHUNK):
            cols = slice(c, c + CHUNK)
            ci = s["proj"][rows, inner + c : inner + c + CHUNK]
            pre = s["pre"][:, cols]
            sg = sigmoid(pre)
            dpre = s["dco"][:, cols] * (sg * (1.0 + pre * (1.0 - sg)))
            small[taps : taps + 1, cols] += jnp.sum(dpre, axis=0, keepdims=True)
            small[taps - 1 : taps, cols] += jnp.sum(dpre * ci, axis=0, keepdims=True)
            dci = chan[taps - 1 : taps, cols] * dpre
            for k in range(1, taps):
                back = dpre * keep[k]
                small[taps - 1 - k : taps - k, cols] += jnp.sum(
                    back * pltpu.roll(ci, k, 0), axis=0, keepdims=True
                )
                dci = dci + chan[taps - 1 - k : taps - k, cols] * pltpu.roll(back, t - k, 0)
            s["dproj"][rows, inner + c : inner + c + CHUNK] = dci.astype(BF16)

    def finish(self, u_ref, dres_ref, w, prm, s, small):
        gain = prm[0][6:7, : self.width]
        dnormed = nt(s["dproj"][...], w["in"][...]) + nt(s["ddt"][...], prm[2][...])
        u = u_ref[...].astype(F32)
        rs = lax.rsqrt(jnp.mean(u * u, axis=-1, keepdims=True) + EPS)
        q = u * rs
        small[6:7, : self.width] += jnp.sum(dnormed * q, axis=0, keepdims=True)
        dq = dnormed * gain
        return dres_ref[...].astype(F32) + rs * (dq - q * jnp.mean(dq * q, axis=-1, keepdims=True))


NAMES = ("e", "proj", "co", "xs", "ys", "gated", "mixed", "normed", "dt")
BACK_NAMES = ("pre", "decay", "stepx", "dy", "dco", "t1", "t2", "normed_t", "mixed_t", "dproj", "ddt")
SMALL_ROWS = 16
GROUPS = 4
CHUNKS = 2
ORDERED = True
DIRECT = (False, False)


def load_weights(layer, plan, packed, w, sems, me):
    copies = []
    own = layer.width // plan.shards
    for i, (ref, (k, first)) in enumerate(zip(packed, plan.parts)):
        owner, rows = lax.bitwise_xor(me, k), ref.shape[0]

        def place(columns, dst, start, which):
            at = pl.ds(pl.multiple_of(start, 16), rows)
            copies.append(pltpu.make_async_copy(ref.at[:, columns], dst.at[at, :], sems.at[which, i]))

        place(slice(0, layer.proj), w["in"], owner * own + first, 0)
        for r in range(layer.inner // layer.width):
            columns = slice(layer.proj + r * layer.width, layer.proj + (r + 1) * layer.width)
            place(columns, w["out"], owner * (layer.inner // plan.shards) + r * own + first, 1 + r)
    for copy in copies:
        copy.start()
    each = 1 + layer.inner // layer.width

    def wait_in():
        for copy in copies[::each]:
            copy.wait()

    def wait_out():
        for i, copy in enumerate(copies):
            if i % each:
                copy.wait()

    return wait_in, wait_out


def fill_spread(layer, ref):
    head = lax.broadcasted_iota(jnp.int32, ref.shape, 0) * layer.head_width
    lane = lax.broadcasted_iota(jnp.int32, ref.shape, 1)
    ref[...] = jnp.where((lane >= head) & (lane < head + layer.head_width), 1.0, 0.0).astype(BF16)


class Plan(NamedTuple):
    shards: int
    parts: tuple


def forward_kernel(layer, micro, plan, section, *refs):
    lens, u_ref, chan, heads_prm, w_dt = refs[:5]
    count = len(plan.parts)
    packed = refs[5 : 5 + count]
    y_ref, w_in, w_out, *scr, sems = refs[5 + count :]
    s = dict(zip(NAMES, scr))
    w = {"in": w_in, "out": w_out}

    @pl.when(lax.axis_index("section") == section)
    def _():
        wait_in, wait_out = load_weights(layer, plan, packed, w, sems, lax.axis_index("shard"))
        prm = (chan, heads_prm, w_dt)
        fill_spread(layer, s["e"])
        layer.normalize(u_ref, prm, s)
        wait_in()
        layer.project(w, prm, s)

        @pl.loop(0, micro)
        def _(m):
            rows = pl.ds(pl.multiple_of(m * layer.tok, layer.tok), layer.tok)
            layer.forward(prm, s, layer.masks(lens, m), rows)

        wait_out()
        y_ref[...] = (u_ref[...].astype(F32) + nn(s["mixed"][...], w["out"][...])).astype(BF16)


def pack_small(layer, n, j, small, ref):
    row = lax.broadcasted_iota(jnp.int32, (SMALL_ROWS, layer.convolved), 0)
    all_rows = small[...]

    def from_owner(v, own):
        return pltpu.roll(v, (layer.convolved - j * own) % layer.convolved, 1) if j else v

    mine = from_owner(all_rows, layer.convolved // n)
    mine = jnp.where(row == 5, from_owner(all_rows, layer.inner // n), mine)
    mine = jnp.where(row == 6, from_owner(all_rows, layer.width // n), mine)
    mine = jnp.where(row >= 7, from_owner(all_rows, layer.heads // n), mine)
    for g in range(GROUPS):
        ref[g * SMALL_ROWS : (g + 1) * SMALL_ROWS, LANES:CHUNK] = mine[
            :, g * LANES : (g + 1) * LANES
        ].astype(BF16)


def both_kernel(layer, micro, plan, section, *refs):
    n = plan.shards
    lens, u_ref, chan, heads_prm, w_dt, dres_ref = refs[:6]
    count = len(plan.parts)
    packed = refs[6 : 6 + count]
    y_ref, din_ref, dlow_ref = refs[6 + count : 9 + count]
    ends = 9 + count + 4 * CHUNKS
    outs = refs[9 + count : ends]
    w_in, w_out, *scr, small, gbuf, sems, gsems = refs[ends:]
    s = dict(zip(NAMES + BACK_NAMES, scr))
    w = {"in": w_in, "out": w_out}
    group = gbuf.shape[1] // (2 * CHUNKS)
    targets = []
    for c in range(CHUNKS):
        keep_a, send_a, keep_b, send_b = outs[4 * c : 4 * c + 4]
        targets.append((keep_a.at[0], send_a.at[0], keep_a.at[1], send_a.at[1]))
        targets.append((keep_b.at[0], keep_b.at[1], send_b.at[0], send_b.at[1]))

    @pl.when(lax.axis_index("section") == section)
    def _():
        me = lax.axis_index("shard")
        wait_in, wait_out = load_weights(layer, plan, packed, w, sems, me)
        prm = (chan, heads_prm, w_dt)
        fill_spread(layer, s["e"])
        small[...] = jnp.zeros(small.shape, F32)
        layer.normalize(u_ref, prm, s)
        wait_in()
        layer.project(w, prm, s)
        wait_out()
        for c in range(0, layer.inner, CHUNK):
            s["dy"][:, c : c + CHUNK] = nt(dres_ref[...], w["out"][c : c + CHUNK, :])

        @pl.loop(0, micro)
        def _(m):
            rows = pl.ds(pl.multiple_of(m * layer.tok, layer.tok), layer.tok)
            masks = layer.masks(lens, m)
            kept = layer.forward(prm, s, masks, rows)
            layer.backward(kept, prm, s, masks, small, rows)

        y_ref[...] = (u_ref[...].astype(F32) + nn(s["mixed"][...], w["out"][...])).astype(BF16)
        din = layer.finish(u_ref, dres_ref, w, prm, s, small)
        din_ref[...] = din
        dlow_ref[...] = din.astype(BF16)
        s["normed_t"][...] = s["normed"][...].astype(F32).T.astype(BF16)
        for c in range(0, layer.inner, CHUNK):
            cols = slice(c, c + CHUNK)
            s["mixed_t"][cols, :] = s["mixed"][:, cols].astype(F32).T.astype(BF16)

        def send_off(which, j):
            for k in range(n):

                @pl.when(lax.bitwise_xor(me, k) == j)
                def _(k=k):
                    pltpu.make_async_copy(
                        gbuf.at[j, which * group : (which + 1) * group], targets[which][k], gsems.at[which, k]
                    ).start()

        in_rows, in_blocks, out_blocks = layer.width // n, layer.proj // CHUNK, layer.width // CHUNK

        def in_block(b):
            grad = nn(s["normed_t"][...], s["dproj"][:, b * CHUNK : (b + 1) * CHUNK])
            for j in range(n):
                gbuf[j, b] = grad[j * in_rows : (j + 1) * in_rows].astype(BF16)

        def out_blocks_of(c):
            for first in range(0, layer.inner, layer.width):
                grad = nn(
                    s["mixed_t"][first : first + layer.width, :], dres_ref[:, c * CHUNK : (c + 1) * CHUNK]
                )
                for i in range(n):
                    j, r = divmod(first // in_rows + i, layer.inner // layer.width)
                    gbuf[j, in_blocks + r * out_blocks + c] = grad[i * in_rows : (i + 1) * in_rows].astype(BF16)

        skip = sum(nt(part, s["e"][...]) for part in split2(small[7:8, : layer.inner]))
        small[7:8, :LANES] = skip
        def last_block(j):
            last = gbuf.at[j, 2 * CHUNKS * group - 1]
            last[...] = jnp.zeros(last.shape, BF16)
            last[:, :LANES] = nn(
                s["normed_t"][j * in_rows : (j + 1) * in_rows, :], s["ddt"][...]
            ).astype(BF16)
            pack_small(layer, n, j, small, last)

        total = gbuf.shape[1]
        for b in range(in_blocks + layer.inner // layer.width * out_blocks, total - 1):
            gbuf[:, b] = jnp.zeros((n,) + gbuf.shape[2:], BF16)
        sent = 0
        for b in range(in_blocks):
            in_block(b)
            if (b + 1) % group == 0:
                for j in range(n):
                    send_off(sent, j)
                sent += 1
        for c in range(out_blocks):
            out_blocks_of(c)
        for j in range(n):
            last_block(j)
        for which in range(sent, 2 * CHUNKS):
            for j in range(n):
                send_off(which, j)
        for which in range(2 * CHUNKS):
            for k in range(n):
                pltpu.make_async_copy(
                    gbuf.at[k, which * group : (which + 1) * group], targets[which][k], gsems.at[which, k]
                ).wait()


VMEM = pl.BlockSpec(memory_space=pltpu.VMEM)
ANY = pl.BlockSpec(memory_space=pl.ANY)


def call_layer(layer, micro, plan, section, backward, lens, u, prm, pieces, dres=None):
    n = plan.shards
    tokens = micro * layer.tok
    smem = pl.BlockSpec(memory_space=pltpu.SMEM)
    scratch = layer.scratch(backward, micro)
    y = jax.ShapeDtypeStruct((tokens, layer.width), BF16)
    work = 2 * tokens * layer.width * (layer.proj + layer.inner)
    cost = pl.CostEstimate(
        flops=work * (4 if backward else 1),
        bytes_accessed=8_000_000 * (2 if backward else 1),
        transcendentals=tokens * layer.tok * layer.heads,
    )
    params = pltpu.CompilerParams(vmem_limit_bytes=VMEM_LIMIT)
    load_sems = pltpu.SemaphoreType.DMA((1 + layer.inner // layer.width, len(plan.parts)))
    if not backward:
        return pl.pallas_call(
            functools.partial(forward_kernel, layer, micro, plan, section),
            out_shape=y,
            in_specs=[smem] + [VMEM] * 4 + [ANY] * len(pieces),
            out_specs=VMEM,
            scratch_shapes=scratch + [load_sems],
            compiler_params=params,
            cost_estimate=cost,
            name="layer_forward",
        )(lens, u, *prm, *pieces)
    blocks = layer.blocks(n)
    packed = jax.ShapeDtypeStruct((2, blocks // (2 * CHUNKS), layer.width // n, CHUNK), BF16)
    return pl.pallas_call(
        functools.partial(both_kernel, layer, micro, plan, section),
        out_shape=[y, jax.ShapeDtypeStruct((tokens, layer.width), F32), y] + [packed] * (4 * CHUNKS),
        in_specs=[smem] + [VMEM] * 5 + [ANY] * len(pieces),
        out_specs=[VMEM] * 3 + [ANY] * (4 * CHUNKS),
        scratch_shapes=scratch
        + [
            pltpu.VMEM((SMALL_ROWS, layer.convolved), F32),
            pltpu.VMEM((n, blocks, layer.width // n, CHUNK), BF16),
            load_sems,
            pltpu.SemaphoreType.DMA((2 * CHUNKS, n)),
        ],
        compiler_params=params,
        cost_estimate=cost,
        name="layer_both",
    )(lens, u, *prm, dres, *pieces)


def copy_all(pairs, sems):
    copies = [pltpu.make_async_copy(src, dst, sems.at[i]) for i, (src, dst) in enumerate(pairs)]
    for copy in copies:
        copy.start()
    for copy in copies:
        copy.wait()


def pack_kernel(w_in, w_out, top, bottom, sems):
    proj, rows, width = w_in.shape[1], w_in.shape[0], w_out.shape[1]
    half = rows // 2
    pairs = []
    for i, out in enumerate((top, bottom)):
        pairs.append((w_in.at[i * half : (i + 1) * half, :], out.at[:, :proj]))
        for r in range(w_out.shape[0] // rows):
            columns = slice(proj + r * width, proj + (r + 1) * width)
            first = r * rows + i * half
            pairs.append((w_out.at[first : first + half, :], out.at[:, columns]))
    copy_all(pairs, sems)


def pack(w_in, w_out):
    groups = w_out.shape[0] // w_in.shape[0]
    half = jax.ShapeDtypeStruct((w_in.shape[0] // 2, w_in.shape[1] + groups * w_out.shape[1]), BF16)
    return pl.pallas_call(
        pack_kernel,
        out_shape=[half, half],
        in_specs=[ANY, ANY],
        out_specs=[VMEM, VMEM],
        scratch_shapes=[pltpu.SemaphoreType.DMA((2 * (1 + groups),))],
        cost_estimate=pl.CostEstimate(flops=0, bytes_accessed=4_000_000, transcendentals=0),
        name="pack",
    )(w_in, w_out)


def hold_kernel(section, count, waits, *refs):
    values, outs = refs[:count], refs[count + waits : 2 * count + waits]
    bufs, sems = refs[2 * count + waits : -1], refs[-1]

    def move():
        copy_all(list(zip(values, bufs)), sems)
        copy_all(list(zip(bufs, outs)), sems)

    if section is None:
        move()
    else:
        pl.when(lax.axis_index("section") == section)(move)


def hold(values, tokens, section=None):
    return pl.pallas_call(
        functools.partial(hold_kernel, section, len(values), len(tokens)),
        out_shape=[jax.ShapeDtypeStruct(v.shape, v.dtype) for v in values],
        in_specs=[ANY] * (len(values) + len(tokens)),
        out_specs=[ANY] * len(values),
        scratch_shapes=[pltpu.VMEM(v.shape, v.dtype) for v in values]
        + [pltpu.SemaphoreType.DMA((len(values),))],
        cost_estimate=pl.CostEstimate(flops=0, bytes_accessed=4_000_000, transcendentals=0),
        name="hold",
    )(*values, *tokens)


def pass_on_kernel(section, keep_a, got_a, keep_b, got_b, *refs):
    out_a, out_b, buf, sems = refs[-4:]

    @pl.when(lax.axis_index("section") == section)
    def _():
        sources = (keep_a, got_a, keep_b, got_b)
        copy_all([(ref.at[1], buf.at[i]) for i, ref in enumerate(sources)], sems)
        for i in range(buf.shape[1]):
            out_a[i] = (buf[0, i].astype(F32) + buf[1, i].astype(F32)).astype(BF16)
            out_b[i] = (buf[2, i].astype(F32) + buf[3, i].astype(F32)).astype(BF16)


def sum_to_pass_on(section, terms, tokens):
    shape = terms[0].shape[1:]
    return pl.pallas_call(
        functools.partial(pass_on_kernel, section),
        out_shape=[jax.ShapeDtypeStruct(shape, BF16)] * 2,
        in_specs=[ANY] * (4 + len(tokens)),
        out_specs=[VMEM] * 2,
        scratch_shapes=[pltpu.VMEM((4,) + shape, BF16), pltpu.SemaphoreType.DMA((4,))],
        cost_estimate=pl.CostEstimate(flops=1_000_000, bytes_accessed=3_000_000, transcendentals=0),
        name="sum_to_pass_on",
    )(*terms, *tokens)


def dp_part(parts, k):
    return lax.bitwise_xor(lax.axis_index("dp") & (parts - 1), k)


def cut_kernel(section, parts, keep_a, got_a, last_a, keep_b, got_b, last_b, *refs):
    outs, (buf, sems) = refs[:parts], refs[parts:]

    @pl.when(lax.axis_index("section") == section)
    def _():
        sources = (keep_a.at[0], got_a.at[0], last_a, keep_b.at[0], got_b.at[0], last_b)
        copies = [
            pltpu.make_async_copy(ref, buf.at[i], sems.at[i]) for i, ref in enumerate(sources)
        ]
        for copy in copies:
            copy.start()
        half, rows = buf.shape[1], buf.shape[2] // parts
        for h in range(2):
            for copy in copies[3 * h : 3 * h + 3]:
                copy.wait()
            for k in range(parts):
                part = pl.ds(pl.multiple_of(dp_part(parts, k) * rows, rows), rows)
                for i in range(half):
                    total = sum(buf[3 * h + t, i, part, :].astype(F32) for t in range(3))
                    outs[k][h * half + i] = total.astype(BF16)


def cut_for_dp(section, parts, operands):
    _, half, rows, columns = operands[0].shape
    return pl.pallas_call(
        functools.partial(cut_kernel, section, parts),
        out_shape=[jax.ShapeDtypeStruct((2 * half, rows // parts, columns), BF16)] * parts,
        in_specs=[ANY] * 6,
        out_specs=[VMEM] * parts,
        scratch_shapes=[
            pltpu.VMEM((6, half, rows, columns), BF16),
            pltpu.SemaphoreType.DMA((6,)),
        ],
        compiler_params=pltpu.CompilerParams(vmem_limit_bytes=VMEM_LIMIT),
        cost_estimate=pl.CostEstimate(flops=5_000_000, bytes_accessed=8_000_000, transcendentals=0),
        name="cut_for_dp",
    )(*operands)


def unpack_kernel(layer, n, counts, *refs):
    sets, at = [], 0
    for count in counts:
        sets.append([refs[at + c * count : at + (c + 1) * count] for c in range(CHUNKS)])
        at += CHUNKS * count
    norm, w_in, w_dt, conv_w, conv_b, dt_bias, a_log, skip, inner, w_out, buf, sems = refs[at:]

    for which, (count, chunks) in enumerate(zip(counts, sets)):

        @pl.when(lax.axis_index("section") == which)
        def _(count=count, chunks=chunks):
            copies = []
            for c in range(CHUNKS):
                for k in range(count):
                    ref = chunks[c][k]
                    blocks, rows = ref.shape[:2]
                    start = pl.multiple_of(dp_part(count, k) * rows, rows)
                    dst = buf.at[c * blocks : (c + 1) * blocks, pl.ds(start, rows), :]
                    copies.append(pltpu.make_async_copy(ref, dst, sems.at[c, k]))
            for copy in copies:
                copy.start()
            for copy in copies:
                copy.wait()

    in_blocks, out_blocks = layer.proj // CHUNK, layer.width // CHUNK
    in_rows = buf.shape[1]
    for b in range(in_blocks):
        w_in[:, b * CHUNK : (b + 1) * CHUNK] = buf[b].astype(F32)
    for r in range(layer.inner // layer.width):
        for c in range(out_blocks):
            w_out[r * in_rows : (r + 1) * in_rows, c * CHUNK : (c + 1) * CHUNK] = buf[
                in_blocks + r * out_blocks + c
            ].astype(F32)
    last = buf.shape[0] - 1
    w_dt[...] = buf[last, :, :LANES].astype(F32).T[: layer.heads, :]

    def channels(row, ref, row_count=1):
        count = ref.shape[1]
        for g in range(-(-count // LANES)):
            lanes = min(LANES, count - g * LANES)
            group = buf[last, g * SMALL_ROWS : (g + 1) * SMALL_ROWS, LANES:CHUNK].astype(F32)
            ref[:, g * LANES : g * LANES + lanes] = group[row : row + row_count, :lanes]

    channels(0, conv_w, layer.taps)
    channels(layer.taps, conv_b)
    channels(5, inner)
    channels(6, norm)
    channels(7, skip)
    channels(8, dt_bias)
    channels(9, a_log)


def unpack(layer, n, first, second):
    counts = (len(first[0]), len(second[0]))
    operands = [part for chunks in (first, second) for chunk in chunks for part in chunk]
    shapes = (
        (1, layer.width // n), (layer.width // n, layer.proj), (layer.heads, layer.width // n),
        (layer.taps, layer.convolved // n), (1, layer.convolved // n), (1, layer.heads // n),
        (1, layer.heads // n), (1, layer.heads // n), (1, layer.inner // n), (layer.inner // n, layer.width),
    )
    return pl.pallas_call(
        functools.partial(unpack_kernel, layer, n, counts),
        out_shape=[jax.ShapeDtypeStruct(shape, F32) for shape in shapes],
        in_specs=[ANY] * len(operands),
        out_specs=[VMEM] * len(shapes),
        scratch_shapes=[
            pltpu.VMEM((layer.blocks(n), layer.width // n, CHUNK), BF16),
            pltpu.SemaphoreType.DMA((CHUNKS, max(counts))),
        ],
        compiler_params=pltpu.CompilerParams(vmem_limit_bytes=VMEM_LIMIT),
        cost_estimate=pl.CostEstimate(flops=0, bytes_accessed=6_000_000, transcendentals=0),
        name="unpack",
    )(*operands)


def exchange(block, axis, distance, section=None):
    size = lax.axis_size(axis)
    if section is None:
        return lax.ppermute(block, axis, [(i, i ^ distance) for i in range(size)])
    base = section * size
    route = [(base + i, base + (i ^ distance)) for i in range(size)]
    return lax.ppermute(block, ("section", axis), route)


def wide_sum(*parts):
    return sum(part.astype(F32) for part in parts)


X_WAY, Y_WAY, BOTH_WAYS = 1, 2, 3


def gather(halves, section):
    top, bottom = halves
    x_top = exchange(top, "shard", X_WAY, section)
    y_bottom = exchange(bottom, "shard", Y_WAY, section)
    x_bottom = exchange(bottom, "shard", X_WAY, section)
    y_top = exchange(top, "shard", Y_WAY, section)
    far_top = exchange(x_top, "shard", Y_WAY, section)
    far_bottom = exchange(y_bottom, "shard", X_WAY, section)
    return x_top, x_bottom, y_top, y_bottom, far_top, far_bottom


def sum_over_shard(packed, section, tokens):
    keep_a, send_a, keep_b, send_b = packed
    got_a = exchange(send_a, "shard", X_WAY, section)
    got_b = exchange(send_b, "shard", Y_WAY, section)
    far_a, far_b = sum_to_pass_on(section, (keep_a, got_a, keep_b, got_b), tokens)
    last_a = exchange(far_a, "shard", Y_WAY, section)
    last_b = exchange(far_b, "shard", X_WAY, section)
    return keep_a, got_a, last_a, keep_b, got_b, last_b


def sum_layer(packed, section):
    done, tokens = [], ()
    for c in range(CHUNKS):
        terms = sum_over_shard(packed[4 * c : 4 * c + 4], section, tokens)
        tokens = (terms[2], terms[5]) if ORDERED else ()
        done.append(sum_over_dp(terms, section, DIRECT[section]))
    return done


def sum_over_dp(terms, section, direct):
    size = lax.axis_size("dp")
    if size != 4:
        [total] = cut_for_dp(section, 1, terms)
        return [lax.psum(total, "dp")]
    if direct:
        parts = cut_for_dp(section, 4, terms)
        got = [exchange(parts[k], "dp", k, section) for k in range(1, 4)]
        done = wide_sum(parts[0], *got).astype(BF16)
        return [done] + [exchange(done, "dp", k, section) for k in range(1, 4)]
    own, other = cut_for_dp(section, 2, terms)
    pair = wide_sum(own, exchange(other, "dp", 1, section)).astype(BF16)
    done = wide_sum(pair, exchange(pair, "dp", 2, section)).astype(BF16)
    return [done, exchange(done, "dp", 1, section)]


def in_order(by_distance, me):
    a, b, c, d = by_distance
    odd, high = (me & 1) != 0, (me & 2) != 0
    a, b = jnp.where(odd, b, a), jnp.where(odd, a, b)
    c, d = jnp.where(odd, d, c), jnp.where(odd, c, d)
    return [jnp.where(high, p, q) for p, q in ((c, a), (d, b), (a, c), (b, d))]


def body(
    tokens_in, seq_lengths, out_grad, norm_gain, w_in, w_dt, conv_w, conv_b,
    dt_bias, a_log, d_skip, inner_gain, w_out,
):
    is_first = lax.axis_index("section") == 0
    shard_pos = lax.axis_index("shard")
    n = lax.axis_size("shard")
    micro, tok, width = tokens_in.shape
    own_heads = dt_bias.shape[1]
    heads, taps = own_heads * n, conv_w.shape[1]
    inner, convolved = inner_gain.shape[1] * n, conv_b.shape[1] * n
    layer = Layer(tok, width, inner, convolved, heads, taps)

    own_conv, own_inner, own_width = conv_b.shape[1], inner_gain.shape[1], norm_gain.shape[1]
    flat = jnp.concatenate(
        [v.reshape(-1) for v in (conv_w, conv_b, inner_gain, norm_gain, dt_bias, a_log, d_skip, w_dt)]
    )
    packed = -(-flat.shape[0] // 2048) * 2048
    flat = jnp.pad(flat, (0, packed - flat.shape[0])).reshape(-1, LANES)
    def parameters(flats):
        everyone = jnp.stack(in_order(flats, shard_pos)).reshape(n, packed)
        at = [0]

        def take(count):
            at[0] += count
            return everyone[:, at[0] - count : at[0]]

        conv_w_all = take(taps * own_conv).reshape(n, taps, own_conv).transpose(1, 0, 2).reshape(taps, convolved)
        conv_b_all = take(own_conv).reshape(1, convolved)
        inner_all = take(own_inner).reshape(1, inner)
        norm_all = take(own_width).reshape(1, width)
        dt_bias_all = take(own_heads).reshape(1, heads)
        a_log_all = take(own_heads).reshape(1, heads)
        d_skip_all = take(own_heads).reshape(1, heads)
        w_dt_all = jnp.pad(take(own_width * heads).reshape(width, heads), ((0, 0), (0, LANES - heads)))

        def padded(row):
            return jnp.pad(row, ((0, 0), (0, convolved - row.shape[1])))

        skip_all = jnp.repeat(d_skip_all, inner // heads, axis=1)
        chan = jnp.concatenate(
            [conv_w_all, conv_b_all, padded(inner_all), padded(norm_all), padded(skip_all)], axis=0
        ).astype(F32)
        heads_prm = jnp.pad(
            jnp.concatenate([dt_bias_all, a_log_all], axis=0), ((0, 6), (0, LANES - heads))
        ).astype(F32)
        return chan, heads_prm, w_dt_all

    half = own_width // 2
    plan = Plan(n, tuple((k, first) for k in (0, X_WAY, Y_WAY, BOTH_WAYS) for first in (0, half)))
    own_w = tuple(pack(w_in[0], w_out[0]))
    near = gather(own_w, 0)
    first_w = own_w + near
    [flat] = hold((flat,), (near[0], near[3]))
    flats = [flat] + [exchange(flat, "shard", k) for k in (X_WAY, Y_WAY, BOTH_WAYS)]
    token = wide_sum(near[0][:16, :LANES], near[3][:16, :LANES]).astype(BF16)
    token = lax.ppermute(token, "section", [(0, 1)])
    second_w = own_w + gather(hold(own_w, (token,), 1), 1)
    prm = parameters(hold(flats, near[1:3]))

    lens = seq_lengths[:, 0, :]
    tokens = tokens_in.reshape(micro * tok, width)
    cotangent = out_grad.reshape(micro * tok, width)
    hidden = call_layer(layer, micro, plan, 0, False, lens, tokens, prm, first_w)
    arrived = lax.ppermute(hidden, "section", [(0, 1)])
    final, second_in_grad, second_low, *second_g = call_layer(
        layer, micro, plan, 1, True, lens, arrived, prm, second_w, dres=cotangent
    )
    back = lax.ppermute(second_low, "section", [(1, 0)])
    _, first_in_grad, _, *first_g = call_layer(
        layer, micro, plan, 0, True, lens, tokens, prm, first_w, dres=back
    )
    second_done = sum_layer(second_g, 1)
    first_done = sum_layer(first_g, 0)
    g_norm, g_w_in, g_w_dt, g_conv_w, g_conv_b, g_dt_bias, g_a_log, g_d_skip, g_inner, g_w_out = unpack(
        layer, n, first_done, second_done
    )

    shape = (1, micro, tok, width)
    section_out = jnp.where(is_first, hidden, final).reshape(shape)
    section_in_grad = jnp.where(is_first, first_in_grad, second_in_grad).reshape(shape)
    return (
        section_out, section_in_grad, g_norm, g_w_in[None], g_w_dt.T[None], g_conv_w[None], g_conv_b,
        g_dt_bias, g_a_log, g_d_skip, g_inner, g_w_out[None],
    )


def solution(mesh):
    spread = P(None, ("dp", "shard"), None)
    flat, tall, conv = P("section", "shard"), P("section", "shard", None), P("section", None, "shard")
    outer = P("section", None, ("dp", "shard"), None)
    return jax.shard_map(
        body,
        mesh=mesh,
        in_specs=(spread, spread, spread, flat, tall, tall, conv, flat, flat, flat, flat, flat, tall),
        out_specs=(outer, outer, flat, tall, tall, conv, flat, flat, flat, flat, flat, tall),
        check_vma=False,
    )
```
